256 devices in a mesh: blk: 64 (over x, z, y_hi), col: 4 (over y_lo, core).
Axes of the slice: x: 4, y: 4 (y_hi: 2, y_lo: 2; y = y_hi * 2 + y_lo), z: 8, core: 2. Of those that a mesh axis runs over, the one named last changes fastest.
Arguments:
- points: bfloat16 [32768, 128], P(('blk', 'col')), may hold values from -4.5 to 4.5
- targets: float32 [32768, 32], P(('blk', 'col')), may hold values from -6 to 6
- pivots: int32 [2, 256], replicated, may hold values from 0 to 32767, as said below
Outputs:
- factor: bfloat16 [32768, 512], P(('blk', 'col'))
- solution: float32 [32768, 32], P(('blk', 'col'))
- residual: float32 [32768, 32], P(('blk', 'col'))
The draws below stay inside these ranges and needn't reach their ends.
Inputs may be any that keep to these rules, and one draw needn't show every extreme that they name: `pivots`: the 512 indices are distinct; 0 and 32767 are among them.
All inputs are finite; a program needn't handle non-finite values.
Results may differ from the reference program's by a relative error of at most 0.012.
Values may be sent and summed in bfloat16 or wider, within the bound.
No kernel may reach another device: no remote copies, remote signals or barrier semaphores. Data moves between devices by JAX's collectives and lax.ppermute only.
A program may use at most 64 MiB of HBM per device.

```python
import jax
import jax.numpy as jnp
from jax import lax

FEATURES = 128
PIV_BLOCK = 256
RHS_COLS = 32
ITERS = 3
POINTS = 32768


def draw_points(key, part):
    row_key, value_key = jax.random.split(key, 2)
    values = jnp.clip(jax.random.normal(value_key, (POINTS, FEATURES), jnp.float32), -4.5, 4.5)
    scales = jnp.exp(jax.random.uniform(row_key, (POINTS,), jnp.float32, jnp.log(0.25), jnp.log(1.0)))
    result = values * scales[:, None]
    return jnp.clip(result, -4.5, 4.5).astype(jnp.bfloat16)


def draw_pivots(key, part):
    first_key, second_key = jax.random.split(jax.random.fold_in(key, 11))
    middle = jax.random.permutation(first_key, POINTS - 2)[:2 * PIV_BLOCK - 2].astype(jnp.int32) + 1
    ends = jnp.array([0, POINTS - 1], dtype=jnp.int32)
    chosen = jnp.concatenate([ends, middle])
    return jax.random.permutation(second_key, chosen).astype(jnp.int32).reshape(2, PIV_BLOCK)


def levels(key, extent, shards, low, largest):
    def one(axis_at, shards_of):
        heights = jax.random.uniform(jax.random.fold_in(jax.random.fold_in(key, 6), axis_at), (shards_of,), jnp.float32, low / len(shards), largest / len(shards))
        return jnp.repeat(jnp.exp(heights), extent[axis_at] // shards_of).reshape((-1,) + (1,) * (len(extent) - axis_at - 1))

    factor_of = one(*shards[0])
    for cut in shards[1:]:
        factor_of = factor_of * one(*cut)
    return factor_of


def noise(own_key, dims, width, bound, cuts=(), held_as=jnp.bfloat16):
    drawn = jax.random.normal(own_key, dims, jnp.float32) * width
    if len(cuts) > 0:
        drawn = levels(own_key, dims, cuts, -0.22, 0.18) * drawn
    return jnp.clip(drawn, min=-bound, max=bound).astype(held_as)


def setup_inputs(seed: int = 0) -> dict:
    keys = jax.random.split(jax.random.key(seed), 4)
    return {
        "points": draw_points(jax.random.fold_in(keys[3], 71), 0),
        "targets": noise(keys[1], (POINTS, RHS_COLS), 1.0, 6.0, ((0, 256),), jnp.float32),
        "pivots": draw_pivots(jax.random.fold_in(keys[3], 71), 0),
    }


noise_level = 0.5
jitter_level = 0.05
highest = lax.Precision.HIGHEST

def squared_norms(point_rows):
    wide_rows = point_rows.astype(jnp.float32)
    return jnp.sum(wide_rows * wide_rows, axis=1)

def kernel_block(left_rows, left_norms, right_rows, right_norms):
    inner = lax.dot_general(left_rows.astype(jnp.float32), right_rows.astype(jnp.float32), (((1,), (1,)), ((), ())), preferred_element_type=jnp.float32)
    distance = left_norms[:, None] + right_norms[None, :] - 2.0 * inner
    return jnp.exp(-2.0 * distance / FEATURES)

def lower_solve(lower_factor, right_rows):
    return jax.scipy.linalg.solve_triangular(lower_factor, right_rows.T, lower=True).T

def build_factor(point_rows, first_pick, second_pick):
    row_norms = squared_norms(point_rows)
    first_norms = squared_norms(first_pick)
    second_norms = squared_norms(second_pick)
    identity_piv = jnp.eye(first_pick.shape[0], dtype=jnp.float32)
    first_chol = jnp.linalg.cholesky(kernel_block(first_pick, first_norms, first_pick, first_norms) + jitter_level * identity_piv)
    first_coef = lower_solve(first_chol, kernel_block(point_rows, row_norms, first_pick, first_norms))
    shared_coef = lower_solve(first_chol, kernel_block(second_pick, second_norms, first_pick, first_norms))
    schur_block = kernel_block(second_pick, second_norms, second_pick, second_norms) + jitter_level * identity_piv - jnp.dot(shared_coef, shared_coef.T, precision=highest)
    second_chol = jnp.linalg.cholesky(schur_block)
    second_cross = kernel_block(point_rows, row_norms, second_pick, second_norms) - jnp.dot(first_coef, shared_coef.T, precision=highest)
    second_coef = lower_solve(second_chol, second_cross)
    return jnp.concatenate([first_coef, second_coef], axis=1)

def reference(points, targets, pivots):
    wide_factor = build_factor(points, points[pivots[0]], points[pivots[1]])
    factor = wide_factor.astype(jnp.bfloat16)
    gram = lax.dot_general(wide_factor, wide_factor, (((0,), (0,)), ((), ())), precision=highest)
    gram = gram + noise_level * jnp.eye(2 * PIV_BLOCK, dtype=jnp.float32)
    gram_chol = jnp.linalg.cholesky(gram)
    row_norms = squared_norms(points)

    def precondition(residual_now):
        projection = lax.dot_general(wide_factor, residual_now, (((0,), (0,)), ((), ())), precision=highest)
        coefficients = jax.scipy.linalg.cho_solve((gram_chol, True), projection)
        return (residual_now - jnp.dot(wide_factor, coefficients, precision=highest)) / noise_level
    block_rows = min(POINTS, 512)
    block_count = POINTS // block_rows

    def kernel_product(directions):

        def one_block(operands):
            weights = kernel_block(operands[0], operands[1], points, row_norms)
            return jnp.dot(weights, directions, precision=highest)
        stacked = lax.map(one_block, (points.reshape(block_count, block_rows, FEATURES), row_norms.reshape(block_count, block_rows)))
        return stacked.reshape(POINTS, RHS_COLS) + noise_level * directions
    solution = jnp.zeros_like(targets)
    residual = targets
    direction_now = precondition(residual)
    inner_now = jnp.sum(residual * direction_now, axis=0)
    for step_index in range(ITERS):
        image = kernel_product(direction_now)
        step_size = inner_now / jnp.sum(direction_now * image, axis=0)
        solution = solution + step_size * direction_now
        residual = residual - step_size * image
        if step_index + 1 < ITERS:
            scaled = precondition(residual)
            inner_next = jnp.sum(residual * scaled, axis=0)
            direction_now = scaled + inner_next / inner_now * direction_now
            inner_now = inner_next
    return (factor, solution, residual)
```

```python
import functools

import jax
import jax.numpy as jnp
import numpy as np
from jax import lax
from jax.experimental import pallas as pl
from jax.experimental.pallas import tpu as pltpu
from jax.sharding import Mesh, PartitionSpec as P

ITERS = 3
NOISE = 0.5
JITTER = 0.05
HIGHEST = lax.Precision.HIGHEST
INTERPRET = False

U = ("z", "yh")
V = ("x", "yl", "c")
ALL = ("x", "z", "yh", "yl", "c")


def swap(blocks, axes):
    return lax.all_to_all(blocks, axes, 0, 0, tiled=False)


def share(block, axes):
    count = lax.axis_size(axes)
    return swap(jnp.broadcast_to(block[None], (count,) + block.shape), axes)


def three_parts(values):
    high = lax.reduce_precision(values, 8, 7)
    rest = values - high
    middle = lax.reduce_precision(rest, 8, 7)
    low = rest - middle
    return [part.astype(jnp.bfloat16) for part in (high, middle, low)]


def augment(rows):
    wide = rows.astype(jnp.float32)
    halves = three_parts(jnp.sum(wide * wide, axis=1, keepdims=True) * (-1.0 / 64.0))
    ones = [jnp.ones_like(halves[0])] * 3
    pad = jnp.zeros((rows.shape[0], 122), jnp.bfloat16)
    left = jnp.concatenate([(wide * 0.03125).astype(jnp.bfloat16)] + halves + ones + [pad], axis=1)
    right = jnp.concatenate([rows] + ones + halves + [pad], axis=1)
    return left, right


def dot_nt(left, right, precision=None):
    return lax.dot_general(
        left, right, (((1,), (1,)), ((), ())), precision=precision, preferred_element_type=jnp.float32
    )


def kernel_of(left, right):
    return jnp.exp(dot_nt(left, right))


def product_body(chunk, key_ref, row_ref, parts_ref, out_ref):
    keys = key_ref.shape[0]
    columns = out_ref.shape[0]
    total = jnp.zeros(out_ref.shape, jnp.float32)
    for start in range(0, keys, chunk):
        values = jnp.exp(dot_nt(key_ref[start:start + chunk, :], row_ref[...]))
        high = values.astype(jnp.bfloat16)
        low = (values - high.astype(jnp.float32)).astype(jnp.bfloat16)
        wide = jnp.dot(parts_ref[:, start:start + chunk], high, preferred_element_type=jnp.float32)
        narrow = jnp.dot(
            parts_ref[:2 * columns, start:start + chunk], low, preferred_element_type=jnp.float32
        )
        total = total + (
            wide[:columns] + wide[columns:2 * columns] + wide[2 * columns:]
            + narrow[:columns] + narrow[columns:]
        )
    out_ref[...] = total


def kernel_product(key_left, row_right, direction):
    keys, depth = key_left.shape
    rows = row_right.shape[0]
    columns = direction.shape[0]
    parts = jnp.concatenate(three_parts(direction), axis=0)
    block = min(256, rows)
    return pl.pallas_call(
        functools.partial(product_body, min(256, keys)),
        grid=(rows // block,),
        in_specs=[
            pl.BlockSpec((keys, depth), lambda i: (0, 0)),
            pl.BlockSpec((block, depth), lambda i: (i, 0)),
            pl.BlockSpec((3 * columns, keys), lambda i: (0, 0)),
        ],
        out_specs=pl.BlockSpec((columns, block), lambda i: (0, i)),
        out_shape=jax.ShapeDtypeStruct((columns, rows), jnp.float32),
        compiler_params=pltpu.CompilerParams(vmem_limit_bytes=32 << 20),
        interpret=INTERPRET,
        name="kernel_product",
    )(key_left, row_right, parts)


def inverse_factor(matrix):
    order = matrix.shape[0]
    lower = jnp.linalg.cholesky(matrix)
    return jax.scipy.linalg.solve_triangular(lower, jnp.eye(order, dtype=jnp.float32), lower=True)


def per_device(points, targets, pivots):
    own = points.shape[0]
    columns = targets.shape[1]
    u_size, v_size = lax.axis_size(U), lax.axis_size(V)
    u_at, v_at = lax.axis_index(U), lax.axis_index(V)
    flat_pivots = pivots.reshape(-1)
    piv = flat_pivots.shape[0]
    lanes = 128

    packed = share(jnp.concatenate([points.astype(jnp.float32), targets.T], axis=0), U)
    key_points = packed[:, :own].astype(jnp.bfloat16).reshape(u_size * own, -1)
    residual = packed[:, own:].transpose(1, 0, 2).reshape(columns, u_size * own)

    sizes = {axis: lax.axis_size(axis) for axis in ALL}
    place = jnp.zeros((), jnp.int32)
    u_rest = jnp.arange(u_size, dtype=jnp.int32)
    u_index = {}
    for axis in reversed(U):
        u_index[axis] = u_rest % sizes[axis]
        u_rest = u_rest // sizes[axis]
    for axis in ALL:
        place = place * sizes[axis] + (u_index[axis] if axis in U else lax.axis_index(axis))
    key_ids = (place[:, None] * own + jnp.arange(own, dtype=jnp.int32)[None, :]).reshape(1, -1)

    owned = (flat_pivots[:, None] == key_ids).astype(jnp.bfloat16)
    held = jnp.dot(owned, key_points, preferred_element_type=jnp.float32).astype(jnp.bfloat16)
    part = piv // v_size
    packed = swap(
        jnp.concatenate(
            [
                jnp.broadcast_to(points[None], (v_size,) + points.shape),
                held.reshape(v_size, part, -1),
            ],
            axis=1,
        ),
        V,
    )
    row_points = packed[:, :own].reshape(v_size * own, -1)
    picked = jnp.sum(packed[:, own:].astype(jnp.float32), axis=0).astype(jnp.bfloat16)
    picked = share(picked, V).reshape(piv, -1)

    piv_left, piv_right = augment(picked)
    key_left, key_right = augment(key_points)
    _, row_right = augment(row_points)

    identity = jnp.eye(piv, dtype=jnp.float32)
    low_inverse = inverse_factor(kernel_of(piv_left, piv_right) + JITTER * identity)

    def wide_of(left):
        return dot_nt(kernel_of(left, piv_right), low_inverse, HIGHEST)

    key_wide = wide_of(key_left)
    factor = lax.dynamic_slice_in_dim(key_wide, u_at * own, own, 0).astype(jnp.bfloat16)

    local_gram = lax.dot_general(
        key_wide, key_wide, (((0,), (0,)), ((), ())), precision=HIGHEST
    )
    local_proj = jnp.dot(residual, key_wide, precision=HIGHEST)
    local_sums = jnp.sum(residual * residual, axis=1)
    tail = jnp.zeros((8 * lanes,), jnp.float32).at[:columns].set(local_sums).reshape(1, 8, lanes)
    packed = swap(
        jnp.concatenate(
            [
                local_gram.reshape(v_size, -1, lanes),
                local_proj.reshape(v_size, -1, lanes),
                jnp.broadcast_to(tail, (v_size, 8, lanes)),
            ],
            axis=1,
        ),
        V,
    )
    packed = share(jnp.sum(packed, axis=0), V)
    gram_rows = piv * piv // v_size // lanes
    proj_rows = columns * piv // v_size // lanes
    gram = packed[:, :gram_rows].reshape(piv, piv) + NOISE * identity
    projection = packed[:, gram_rows:gram_rows + proj_rows].reshape(columns, piv)
    squares = packed[0, gram_rows + proj_rows:].reshape(-1)[:columns]
    gram_inverse = inverse_factor(gram)

    def gram_solve(proj):
        return jnp.dot(dot_nt(proj, gram_inverse, HIGHEST), gram_inverse, precision=HIGHEST)

    def precondition(res, coef):
        return (res - dot_nt(coef, key_wide, HIGHEST)) / NOISE

    def own_part(values):
        return lax.dynamic_slice_in_dim(values, u_at * own, own, 1)

    coefficients = gram_solve(projection)
    direction = precondition(residual, coefficients)
    inner = (squares - jnp.sum(projection * coefficients, axis=1)) / NOISE
    solution_own = jnp.zeros((columns, own), jnp.float32)
    for step in range(ITERS):
        last = step + 1 == ITERS
        direction_own = own_part(direction)
        partial = kernel_product(key_left, row_right, direction)
        blocks = partial.reshape(columns, v_size, own).transpose(1, 0, 2)
        image_own = jnp.sum(swap(blocks, V), axis=0) + NOISE * direction_own
        if last:
            curve = jnp.sum(direction_own * image_own, axis=1)
            curve = jnp.zeros((8 * lanes,), jnp.float32).at[:columns].set(curve).reshape(8, lanes)
            curve = jnp.sum(share(curve, V), axis=0)
            curve = jnp.sum(share(curve, U), axis=0)
            alpha = (inner / curve.reshape(-1)[:columns])[:, None]
            solution_own = solution_own + alpha * direction_own
            residual_own = own_part(residual) - alpha * image_own
            break
        image = share(image_own, U).transpose(1, 0, 2).reshape(columns, u_size * own)
        image_proj = jnp.dot(image, key_wide, precision=HIGHEST)
        sums = jnp.concatenate(
            [
                jnp.sum(direction * image, axis=1),
                jnp.sum(residual * image, axis=1),
                jnp.sum(image * image, axis=1),
            ]
        )
        sums = jnp.zeros((8 * lanes,), jnp.float32).at[:3 * columns].set(sums).reshape(8, lanes)
        packed = jnp.sum(
            share(jnp.concatenate([image_proj.reshape(-1, lanes), sums], axis=0), V), axis=0
        )
        image_proj = packed[:-8].reshape(columns, piv)
        sums = packed[-8:].reshape(-1)
        curve, cross, image_squares = (
            sums[:columns], sums[columns:2 * columns], sums[2 * columns:3 * columns]
        )
        alpha = inner / curve
        squares = squares - 2.0 * alpha * cross + alpha * alpha * image_squares
        solution_own = solution_own + alpha[:, None] * direction_own
        residual = residual - alpha[:, None] * image
        projection = projection - alpha[:, None] * image_proj
        coefficients = gram_solve(projection)
        inner_next = (squares - jnp.sum(projection * coefficients, axis=1)) / NOISE
        beta = (inner_next / inner)[:, None]
        inner = inner_next
        direction = precondition(residual, coefficients) + beta * direction
    return (factor, solution_own.T, residual_own.T)


def solution(mesh):
    shape = mesh.devices.shape
    if shape == (64, 4):
        grid = Mesh(mesh.devices.reshape(4, 8, 2, 2, 2), ALL)
    else:
        grid = Mesh(mesh.devices.reshape(2, 2, 2, 2, 1), ALL)
    return jax.shard_map(
        per_device,
        mesh=grid,
        in_specs=(P(ALL, None), P(ALL, None), P()),
        out_specs=(P(ALL, None), P(ALL, None), P(ALL, None)),
        check_vma=False,
    )
```

```python
import functools

import jax
import jax.numpy as jnp
import numpy as np
from jax import lax
from jax.experimental import pallas as pl
from jax.experimental.pallas import tpu as pltpu
from jax.sharding import Mesh, PartitionSpec as P

ITERS = 3
NOISE = 0.5
JITTER = 0.05
HIGHEST = lax.Precision.HIGHEST
INTERPRET = False

U = ("z", "yh")
V = ("x", "yl", "c")
ALL = ("x", "z", "yh", "yl", "c")


def swap(blocks, axes):
    return lax.all_to_all(blocks, axes, 0, 0, tiled=False)


def share(block, axes):
    count = lax.axis_size(axes)
    return swap(jnp.broadcast_to(block[None], (count,) + block.shape), axes)


def partner(values):
    return lax.ppermute(values, "c", [(0, 1), (1, 0)])


def reduce_blocks(blocks):
    pairs = blocks.reshape((-1, 2) + blocks.shape[1:])
    first = lax.axis_index("c") == 0
    mine = jnp.where(first, pairs[:, 0], pairs[:, 1])
    other = jnp.where(first, pairs[:, 1], pairs[:, 0])
    return jnp.sum(swap(mine + partner(other), V[:2]), axis=0)


def gather_blocks(block):
    mine = share(block, V[:2])
    other = partner(mine)
    first = lax.axis_index("c") == 0
    both = jnp.stack([jnp.where(first, mine, other), jnp.where(first, other, mine)], axis=1)
    return both.reshape((-1,) + block.shape)


def sum_over_v(block):
    return jnp.sum(share(block + partner(block), V[:2]), axis=0)


def three_parts(values):
    high = lax.reduce_precision(values, 8, 7)
    rest = values - high
    middle = lax.reduce_precision(rest, 8, 7)
    low = rest - middle
    return [part.astype(jnp.bfloat16) for part in (high, middle, low)]


def augment(rows):
    wide = rows.astype(jnp.float32)
    halves = three_parts(jnp.sum(wide * wide, axis=1, keepdims=True) * (-1.0 / 64.0))
    ones = [jnp.ones_like(halves[0])] * 3
    pad = jnp.zeros((rows.shape[0], 122), jnp.bfloat16)
    left = jnp.concatenate([(wide * 0.03125).astype(jnp.bfloat16)] + halves + ones + [pad], axis=1)
    right = jnp.concatenate([rows] + ones + halves + [pad], axis=1)
    return left, right


def dot_nt(left, right, precision=None):
    return lax.dot_general(
        left, right, (((1,), (1,)), ((), ())), precision=precision, preferred_element_type=jnp.float32
    )


def kernel_of(left, right):
    return jnp.exp(dot_nt(left, right))


def product_body(chunk, key_ref, row_ref, parts_ref, out_ref):
    keys = key_ref.shape[0]
    columns = out_ref.shape[0]
    total = jnp.zeros(out_ref.shape, jnp.float32)
    for start in range(0, keys, chunk):
        values = jnp.exp(dot_nt(key_ref[start:start + chunk, :], row_ref[...]))
        high = values.astype(jnp.bfloat16)
        low = (values - high.astype(jnp.float32)).astype(jnp.bfloat16)
        wide = jnp.dot(parts_ref[:, start:start + chunk], high, preferred_element_type=jnp.float32)
        narrow = jnp.dot(
            parts_ref[:2 * columns, start:start + chunk], low, preferred_element_type=jnp.float32
        )
        total = total + (
            wide[:columns] + wide[columns:2 * columns] + wide[2 * columns:]
            + narrow[:columns] + narrow[columns:]
        )
    out_ref[...] = total


def kernel_product(key_left, row_right, direction):
    keys, depth = key_left.shape
    rows = row_right.shape[0]
    columns = direction.shape[0]
    parts = jnp.concatenate(three_parts(direction), axis=0)
    block = min(256, rows)
    return pl.pallas_call(
        functools.partial(product_body, min(256, keys)),
        grid=(rows // block,),
        in_specs=[
            pl.BlockSpec((keys, depth), lambda i: (0, 0)),
            pl.BlockSpec((block, depth), lambda i: (i, 0)),
            pl.BlockSpec((3 * columns, keys), lambda i: (0, 0)),
        ],
        out_specs=pl.BlockSpec((columns, block), lambda i: (0, i)),
        out_shape=jax.ShapeDtypeStruct((columns, rows), jnp.float32),
        compiler_params=pltpu.CompilerParams(vmem_limit_bytes=32 << 20),
        interpret=INTERPRET,
        name="kernel_product",
    )(key_left, row_right, parts)


GROUP = 8
STRIDE = 8

def eliminate(groups):
    order = len(groups) * GROUP
    lane = lax.broadcasted_iota(jnp.int32, (GROUP, order), 1)
    sub = lax.broadcasted_iota(jnp.int32, (GROUP, order), 0)
    groups = list(groups)
    for first in range(0, order, STRIDE):
        at = first // GROUP
        cols = [None] * len(groups)
        for g in range(at, len(groups)):
            cols[g] = [
                jnp.broadcast_to(groups[g][:, first + j:first + j + 1], (GROUP, order))
                for j in range(STRIDE)
            ]
        home = groups[at]
        own = cols[at]
        rows, inverses, steps = [], [], []
        for j in range(STRIDE):
            r = first % GROUP + j
            inverse = 1.0 / jnp.broadcast_to(own[j][r:r + 1, :], (GROUP, order))
            mult = jnp.where(sub > r, own[j] * inverse, 0.0)
            steps.append([jnp.broadcast_to(own[l][r:r + 1, :], (GROUP, order)) for l in range(j + 1, STRIDE)])
            for l in range(j + 1, STRIDE):
                own[l] = own[l] - mult * steps[j][l - j - 1]
            row = jnp.where(lane == first + j, 1.0, jnp.broadcast_to(home[r:r + 1, :], (GROUP, order)))
            home = jnp.where((lane == first + j) & (sub > r), 0.0, home) - mult * row
            rows.append(jnp.where((lane > first + j) & (lane < first + STRIDE), 0.0, row))
            inverses.append(inverse)
        groups[at] = home
        for g in range(at + 1, len(groups)):
            col = cols[g]
            value = jnp.where((lane >= first) & (lane < first + STRIDE), 0.0, groups[g])
            for j in range(STRIDE):
                mult = col[j] * inverses[j]
                for l in range(j + 1, STRIDE):
                    col[l] = col[l] - mult * steps[j][l - j - 1]
                value = value - mult * rows[j]
            groups[g] = value
    return groups


def inverse_factor_body(block, in_ref, out_ref, work_ref):
    order = in_ref.shape[0]
    work_ref[...] = in_ref[...]

    def stage(j, carry):
        start = pl.multiple_of(j * block, block)
        here = pl.ds(start, block)
        diag = work_ref[here, here]
        groups = eliminate([diag[g:g + GROUP, :] for g in range(0, block, GROUP)])
        done = jnp.concatenate(groups, axis=0)
        row = lax.broadcasted_iota(jnp.int32, (block, block), 0)
        col = lax.broadcasted_iota(jnp.int32, (block, block), 1)
        pivots = jnp.sum(jnp.where(row == col, done, 0.0), axis=1, keepdims=True)
        unit = jnp.where(col < row, done, jnp.where(col == row, 1.0, 0.0))
        local = unit * lax.rsqrt(pivots)
        strip = jnp.dot(local, work_ref[here, :], precision=HIGHEST, preferred_element_type=jnp.float32)
        work_ref[here, :] = strip
        low = lax.dot_general(work_ref[:, here], local, (((1,), (1,)), ((), ())), precision=HIGHEST, preferred_element_type=jnp.float32)
        low = jnp.where(lax.broadcasted_iota(jnp.int32, (order, block), 0) >= start + block, low, 0.0)
        work_ref[here, here] = local
        strip = work_ref[here, :]
        below = lax.broadcasted_iota(jnp.int32, (order, block), 0) >= start + block
        work_ref[:, here] = jnp.where(below, 0.0, work_ref[:, here])
        work_ref[...] = work_ref[...] - jnp.dot(low, strip, precision=HIGHEST, preferred_element_type=jnp.float32)
        return carry

    lax.fori_loop(0, order // block, stage, 0)
    row = lax.broadcasted_iota(jnp.int32, (order, order), 0)
    col = lax.broadcasted_iota(jnp.int32, (order, order), 1)
    out_ref[...] = jnp.where(col <= row, work_ref[...], 0.0)


def inverse_factor(matrix):
    order = matrix.shape[0]
    if INTERPRET:
        return jnp.linalg.inv(jnp.linalg.cholesky(matrix))
    return pl.pallas_call(
        functools.partial(inverse_factor_body, 128),
        out_shape=jax.ShapeDtypeStruct((order, order), jnp.float32),
        scratch_shapes=[pltpu.VMEM((order, order), jnp.float32)],
        compiler_params=pltpu.CompilerParams(vmem_limit_bytes=32 << 20),
        name="inverse_factor",
    )(matrix)


def per_device(points, targets, pivots):
    own = points.shape[0]
    columns = targets.shape[1]
    u_size, v_size = lax.axis_size(U), lax.axis_size(V)
    u_at, v_at = lax.axis_index(U), lax.axis_index(V)
    flat_pivots = pivots.reshape(-1)
    piv = flat_pivots.shape[0]
    lanes = 128

    packed = share(jnp.concatenate([points] + three_parts(targets.T), axis=0), U)
    key_points = packed[:, :own].reshape(u_size * own, -1)
    parts = packed[:, own:].astype(jnp.float32).reshape(u_size, 3, columns, own)
    residual = (parts[:, 0] + parts[:, 1] + parts[:, 2]).transpose(1, 0, 2).reshape(columns, -1)

    sizes = {axis: lax.axis_size(axis) for axis in ALL}
    place = jnp.zeros((), jnp.int32)
    u_rest = jnp.arange(u_size, dtype=jnp.int32)
    u_index = {}
    for axis in reversed(U):
        u_index[axis] = u_rest % sizes[axis]
        u_rest = u_rest // sizes[axis]
    for axis in ALL:
        place = place * sizes[axis] + (u_index[axis] if axis in U else lax.axis_index(axis))
    key_ids = (place[:, None] * own + jnp.arange(own, dtype=jnp.int32)[None, :]).reshape(1, -1)

    owned = (flat_pivots[:, None] == key_ids).astype(jnp.bfloat16)
    held = jnp.dot(owned, key_points, preferred_element_type=jnp.float32).astype(jnp.bfloat16)
    part = piv // v_size
    packed = swap(
        jnp.concatenate(
            [
                jnp.broadcast_to(points[None], (v_size,) + points.shape),
                held.reshape(v_size, part, -1),
            ],
            axis=1,
        ),
        V,
    )
    row_points = packed[:, :own].reshape(v_size * own, -1)
    picked = jnp.sum(packed[:, own:].astype(jnp.float32), axis=0).astype(jnp.bfloat16)
    picked = share(picked, V).reshape(piv, -1)

    piv_left, piv_right = augment(picked)
    key_left, key_right = augment(key_points)
    _, row_right = augment(row_points)

    identity = jnp.eye(piv, dtype=jnp.float32)
    low_inverse = inverse_factor(kernel_of(piv_left, piv_right) + JITTER * identity)

    def wide_of(left):
        return dot_nt(kernel_of(left, piv_right), low_inverse, HIGHEST)

    key_wide = wide_of(key_left)
    factor = lax.dynamic_slice_in_dim(key_wide, u_at * own, own, 0).astype(jnp.bfloat16)

    local_gram = lax.dot_general(
        key_wide, key_wide, (((0,), (0,)), ((), ())), precision=HIGHEST
    )
    local_proj = jnp.dot(residual, key_wide, precision=HIGHEST)
    local_sums = jnp.sum(residual * residual, axis=1)
    tail = jnp.zeros((8 - columns // v_size, piv), jnp.float32).at[0, :columns].set(local_sums)
    packed = reduce_blocks(
        jnp.concatenate(
            [
                local_gram.reshape(v_size, part, piv),
                local_proj.reshape(v_size, columns // v_size, piv),
                jnp.broadcast_to(tail, (v_size,) + tail.shape),
            ],
            axis=1,
        )
    )
    packed = gather_blocks(packed)
    gram = packed[:, :part].reshape(piv, piv) + NOISE * identity
    projection = packed[:, part:part + columns // v_size].reshape(columns, piv)
    squares = packed[0, part + columns // v_size, :columns]
    gram_inverse = inverse_factor(gram)

    def gram_solve(proj):
        return jnp.dot(dot_nt(proj, gram_inverse, HIGHEST), gram_inverse, precision=HIGHEST)

    def precondition(res, coef):
        return (res - dot_nt(coef, key_wide, HIGHEST)) / NOISE

    def own_part(values):
        return lax.dynamic_slice_in_dim(values, u_at * own, own, 1)

    coefficients = gram_solve(projection)
    direction = precondition(residual, coefficients)
    inner = (squares - jnp.sum(projection * coefficients, axis=1)) / NOISE
    solution_own = jnp.zeros((columns, own), jnp.float32)
    for step in range(ITERS):
        last = step + 1 == ITERS
        direction_own = own_part(direction)
        partial = kernel_product(key_left, row_right, direction)
        blocks = partial.reshape(columns, v_size, own).transpose(1, 0, 2)
        image_own = jnp.sum(swap(blocks, V), axis=0) + NOISE * direction_own
        if last:
            curve = jnp.sum(direction_own * image_own, axis=1)
            curve = jnp.zeros((1, lanes), jnp.float32).at[0, :columns].set(curve)
            curve = jnp.sum(share(curve, ALL), axis=0)
            alpha = (inner / curve.reshape(-1)[:columns])[:, None]
            solution_own = solution_own + alpha * direction_own
            residual_own = own_part(residual) - alpha * image_own
            break
        image = share(image_own, U).transpose(1, 0, 2).reshape(columns, u_size * own)
        image_proj = jnp.dot(image, key_wide, precision=HIGHEST)
        sums = jnp.concatenate(
            [
                jnp.sum(direction * image, axis=1),
                jnp.sum(residual * image, axis=1),
                jnp.sum(image * image, axis=1),
            ]
        )
        sums = jnp.zeros((8, piv), jnp.float32).at[0, :3 * columns].set(sums)
        packed = sum_over_v(jnp.concatenate([image_proj, sums], axis=0))
        image_proj = packed[:columns]
        sums = packed[columns]
        curve, cross, image_squares = (
            sums[:columns], sums[columns:2 * columns], sums[2 * columns:3 * columns]
        )
        alpha = inner / curve
        squares = squares - 2.0 * alpha * cross + alpha * alpha * image_squares
        solution_own = solution_own + alpha[:, None] * direction_own
        residual = residual - alpha[:, None] * image
        projection = projection - alpha[:, None] * image_proj
        coefficients = gram_solve(projection)
        inner_next = (squares - jnp.sum(projection * coefficients, axis=1)) / NOISE
        beta = (inner_next / inner)[:, None]
        inner = inner_next
        direction = precondition(residual, coefficients) + beta * direction
    return (factor, solution_own.T, residual_own.T)


def solution(mesh):
    shape = mesh.devices.shape
    if shape == (64, 4):
        grid = Mesh(mesh.devices.reshape(4, 8, 2, 2, 2), ALL)
    else:
        grid = Mesh(mesh.devices.reshape(2, 2, 1, 2, 2), ALL)
    return jax.shard_map(
        per_device,
        mesh=grid,
        in_specs=(P(ALL, None), P(ALL, None), P()),
        out_specs=(P(ALL, None), P(ALL, None), P(ALL, None)),
        check_vma=False,
    )
```

```python
import functools

import jax
import jax.numpy as jnp
from jax import lax
from jax.experimental import pallas as pl
from jax.experimental.pallas import tpu as pltpu
from jax.sharding import Mesh, PartitionSpec as P

ITERS = 3
NOISE = 0.5
JITTER = 0.05
HIGHEST = lax.Precision.HIGHEST
INTERPRET = False
GROUP = 8
STRIDE = 8
BLOCK = 128
F32 = jnp.float32
BF16 = jnp.bfloat16

U = ("z",)
CHIPS = ("x", "yh", "yl")
ALL = ("x", "z", "yh", "yl", "c")


def swap(blocks, axes):
    return lax.all_to_all(blocks, axes, 0, 0, tiled=False)


def share(block, axes):
    count = lax.axis_size(axes)
    return swap(jnp.broadcast_to(block[None], (count,) + block.shape), axes)


def partner(values):
    return lax.ppermute(values, "c", [(0, 1), (1, 0)])


def core_first(mine, other):
    first = lax.axis_index("c") == 0
    return jnp.concatenate([jnp.where(first, mine, other), jnp.where(first, other, mine)], axis=0)


def half(values, at):
    count = values.shape[0] // 2
    return lax.dynamic_slice_in_dim(values, at * count, count, 0)


def three_parts(values):
    high = lax.reduce_precision(values, 8, 7)
    rest = values - high
    middle = lax.reduce_precision(rest, 8, 7)
    low = rest - middle
    return [part.astype(BF16) for part in (high, middle, low)]


def augment(rows):
    wide = rows.astype(F32)
    halves = three_parts(jnp.sum(wide * wide, axis=1, keepdims=True) * (-1.0 / 64.0))
    ones = [jnp.ones_like(halves[0])] * 3
    pad = jnp.zeros((rows.shape[0], 122), BF16)
    left = jnp.concatenate([(wide * 0.03125).astype(BF16)] + halves + ones + [pad], axis=1)
    right = jnp.concatenate([rows] + ones + halves + [pad], axis=1)
    return left, right


def dot_nt(left, right, precision=None):
    return lax.dot_general(
        left, right, (((1,), (1,)), ((), ())), precision=precision, preferred_element_type=F32
    )


def dot_nn(left, right, precision=None):
    return lax.dot_general(
        left, right, (((1,), (0,)), ((), ())), precision=precision, preferred_element_type=F32
    )


def split(values):
    high = values.astype(BF16)
    rest = values - high.astype(F32)
    middle = rest.astype(BF16)
    return high, middle, (rest - middle.astype(F32)).astype(BF16)


def stacked_dot(dot, values, wide):
    count = values.shape[0]
    parts = jnp.concatenate(split(values), axis=0)
    a = dot(parts, wide[0])
    b = dot(parts[:2 * count], wide[1])
    c = dot(parts[:count], wide[2])
    return a[:count] + ((a[count:2 * count] + b[:count]) + (a[2 * count:] + b[count:] + c))


def eliminate(groups):
    order = len(groups) * GROUP
    lane = lax.broadcasted_iota(jnp.int32, (GROUP, order), 1)
    sub = lax.broadcasted_iota(jnp.int32, (GROUP, order), 0)
    groups = list(groups)
    for first in range(0, order, STRIDE):
        at = first // GROUP
        cols = [None] * len(groups)
        for g in range(at, len(groups)):
            cols[g] = [
                jnp.broadcast_to(groups[g][:, first + j:first + j + 1], (GROUP, order))
                for j in range(STRIDE)
            ]
        home = groups[at]
        own = cols[at]
        rows, inverses, steps = [], [], []
        for j in range(STRIDE):
            r = first % GROUP + j
            inverse = 1.0 / jnp.broadcast_to(own[j][r:r + 1, :], (GROUP, order))
            mult = jnp.where(sub > r, own[j] * inverse, 0.0)
            steps.append(
                [
                    jnp.broadcast_to(own[l][r:r + 1, :], (GROUP, order))
                    for l in range(j + 1, STRIDE)
                ]
            )
            for l in range(j + 1, STRIDE):
                own[l] = own[l] - mult * steps[j][l - j - 1]
            row = jnp.where(
                lane == first + j, 1.0, jnp.broadcast_to(home[r:r + 1, :], (GROUP, order))
            )
            home = jnp.where((lane == first + j) & (sub > r), 0.0, home) - mult * row
            rows.append(jnp.where((lane > first + j) & (lane < first + STRIDE), 0.0, row))
            inverses.append(inverse)
        groups[at] = home
        for g in range(at + 1, len(groups)):
            col = cols[g]
            value = jnp.where((lane >= first) & (lane < first + STRIDE), 0.0, groups[g])
            for j in range(STRIDE):
                mult = col[j] * inverses[j]
                for l in range(j + 1, STRIDE):
                    col[l] = col[l] - mult * steps[j][l - j - 1]
                value = value - mult * rows[j]
            groups[g] = value
    return groups


def inverse_of_block(diag):
    if INTERPRET:
        return jnp.linalg.inv(jnp.linalg.cholesky(diag))
    groups = eliminate([diag[g:g + GROUP, :] for g in range(0, BLOCK, GROUP)])
    done = jnp.concatenate(groups, axis=0)
    row = lax.broadcasted_iota(jnp.int32, (BLOCK, BLOCK), 0)
    col = lax.broadcasted_iota(jnp.int32, (BLOCK, BLOCK), 1)
    pivots = jnp.sum(jnp.where(row == col, done, 0.0), axis=1, keepdims=True)
    unit = jnp.where(col < row, done, jnp.where(col == row, 1.0, 0.0))
    return unit * lax.rsqrt(pivots)


def inverse_factor(work_ref):
    order = work_ref.shape[0]

    def stage(j, carry):
        start = pl.multiple_of(j * BLOCK, BLOCK)
        here = pl.ds(start, BLOCK)
        below = lax.broadcasted_iota(jnp.int32, (order, BLOCK), 0) >= start + BLOCK
        local = inverse_of_block(work_ref[here, here])
        work_ref[here, :] = dot_nn(local, work_ref[here, :], HIGHEST)
        low = jnp.where(below, dot_nt(work_ref[:, here], local, HIGHEST), 0.0)
        work_ref[here, here] = local
        strip = work_ref[here, :]
        work_ref[:, here] = jnp.where(below, 0.0, work_ref[:, here])
        work_ref[...] = work_ref[...] - dot_nn(low, strip, HIGHEST)
        return carry

    lax.fori_loop(0, order // BLOCK, stage, 0)
    row = lax.broadcasted_iota(jnp.int32, (order, order), 0)
    col = lax.broadcasted_iota(jnp.int32, (order, order), 1)
    return jnp.where(col <= row, work_ref[...], 0.0)


def unit_matrix(order, scale):
    row = lax.broadcasted_iota(jnp.int32, (order, order), 0)
    col = lax.broadcasted_iota(jnp.int32, (order, order), 1)
    return jnp.where(row == col, scale, 0.0)


def joined(ref):
    return jnp.concatenate([ref[i] for i in range(ref.shape[0])], axis=1)


def setup_body(pl_ref, pr_ref, key_ref, targets_ref, high_ref, mid_ref, low_ref, out_ref, work_ref):
    piv = pl_ref.shape[0]
    chunks, _, _ = out_ref.shape
    part = piv // chunks
    work_ref[...] = jnp.exp(dot_nt(pl_ref[...], pr_ref[...])) + unit_matrix(piv, JITTER)
    inverse = inverse_factor(work_ref)
    wide = dot_nt(jnp.exp(dot_nt(key_ref[...], pr_ref[...])), inverse, HIGHEST)
    parts = split(wide)
    high_ref[...] = parts[0]
    mid_ref[...] = parts[1]
    low_ref[...] = parts[2]
    gram = lax.dot_general(
        wide, wide, (((0,), (0,)), ((), ())), precision=HIGHEST, preferred_element_type=F32
    )
    targets = joined(targets_ref)
    proj = dot_nn(targets, wide, HIGHEST)
    squares = jnp.broadcast_to(jnp.sum(targets * targets, axis=1, keepdims=True), proj.shape)
    per = proj.shape[0] // chunks
    for i in range(chunks):
        out_ref[i, 0:part, :] = gram[i * part:(i + 1) * part, :]
        out_ref[i, part:part + per, :] = proj[i * per:(i + 1) * per, :]
        out_ref[i, part + per:part + 2 * per, :] = squares[i * per:(i + 1) * per, :]


def gram_solve(proj, inverse):
    return dot_nn(dot_nt(proj, inverse, HIGHEST), inverse, HIGHEST)


def product(direction, key_ref, row_ref, out_ref):
    keys = key_ref.shape[0]
    count = direction.shape[0]
    parts = jnp.concatenate(split(direction), axis=0)
    chunk = 256

    def rows_step(i, carry):
        rows = row_ref[pl.ds(pl.multiple_of(i * chunk, chunk), chunk), :]
        total = jnp.zeros((count, chunk), F32)
        for start in range(0, keys, chunk):
            values = jnp.exp(dot_nt(key_ref[start:start + chunk, :], rows))
            high = values.astype(BF16)
            low = (values - high.astype(F32)).astype(BF16)
            a = dot_nn(parts[:, start:start + chunk], high)
            b = dot_nn(parts[:2 * count, start:start + chunk], low)
            total = total + (
                a[:count] + ((a[count:2 * count] + b[:count]) + (a[2 * count:] + b[count:]))
            )
        for k in range(chunk // BLOCK):
            out_ref[i * (chunk // BLOCK) + k] = total[:, k * BLOCK:(k + 1) * BLOCK]
        return carry

    lax.fori_loop(0, row_ref.shape[0] // chunk, rows_step, 0)


def next_direction(residual, coef, wide):
    return (residual - stacked_dot(dot_nt, coef, wide)) * (1.0 / NOISE)


def begin_body(
    packed_ref, res_ref, high_ref, mid_ref, low_ref, key_ref, row_ref,
    inv_ref, proj_ref, dir_ref, inner_ref, sq_ref, out_ref, work_ref,
):
    piv = work_ref.shape[0]
    chunks = packed_ref.shape[0]
    part = piv // chunks
    per = proj_ref.shape[0] // chunks
    for i in range(chunks):
        work_ref[i * part:(i + 1) * part, :] = packed_ref[i, 0:part, :]
        proj_ref[i * per:(i + 1) * per, :] = packed_ref[i, part:part + per, :]
        sq_ref[i * per:(i + 1) * per, :] = packed_ref[i, part + per:part + 2 * per, 0:BLOCK]
    work_ref[...] = work_ref[...] + unit_matrix(piv, NOISE)
    inverse = inverse_factor(work_ref)
    inv_ref[...] = inverse
    proj = proj_ref[...]
    coef = gram_solve(proj, inverse)
    inner_ref[...] = (sq_ref[...] - jnp.sum(proj * coef, axis=1, keepdims=True)) * (1.0 / NOISE)
    direction = next_direction(joined(res_ref), coef, (high_ref[...], mid_ref[...], low_ref[...]))
    for i in range(dir_ref.shape[0]):
        dir_ref[i] = direction[:, i * BLOCK:(i + 1) * BLOCK]
    product(direction, key_ref, row_ref, out_ref)


def project_body(image_ref, res_ref, dir_ref, high_ref, mid_ref, low_ref, out_ref):
    image = joined(image_ref)
    residual = joined(res_ref)
    direction = joined(dir_ref)
    piv = high_ref.shape[1]
    out_ref[:, :piv] = stacked_dot(dot_nn, image, (high_ref[...], mid_ref[...], low_ref[...]))
    curve = jnp.sum(direction * image, axis=1, keepdims=True)
    cross = jnp.sum(residual * image, axis=1, keepdims=True)
    own = jnp.sum(image * image, axis=1, keepdims=True)
    lane = lax.broadcasted_iota(jnp.int32, (image.shape[0], BLOCK), 1)
    out_ref[:, piv:] = jnp.where(lane == 0, curve, jnp.where(lane == 1, cross, own))


def advance_body(
    packed_ref, image_ref, res_ref, dir_ref, sol_ref, proj_ref, inner_ref, sq_ref,
    inv_ref, high_ref, mid_ref, low_ref, key_ref, row_ref,
    new_res, new_dir, new_sol, new_proj, new_inner, new_sq, out_ref,
):
    piv = proj_ref.shape[1]
    total = packed_ref[0]
    for i in range(1, packed_ref.shape[0]):
        total = total + packed_ref[i]
    inner = inner_ref[:, 0:1]
    alpha = inner / total[:, piv:piv + 1]
    squares = (
        sq_ref[:, 0:1] - 2.0 * alpha * total[:, piv + 1:piv + 2]
        + alpha * alpha * total[:, piv + 2:piv + 3]
    )
    proj = proj_ref[...] - alpha * total[:, :piv]
    coef = gram_solve(proj, inv_ref[...])
    inner_next = (squares - jnp.sum(proj * coef, axis=1, keepdims=True)) * (1.0 / NOISE)
    beta = inner_next / inner
    new_proj[...] = proj
    new_inner[...] = jnp.broadcast_to(inner_next, new_inner.shape)
    new_sq[...] = jnp.broadcast_to(squares, new_sq.shape)
    direction = joined(dir_ref)
    residual = joined(res_ref) - alpha * joined(image_ref)
    solution = joined(sol_ref) + alpha * direction
    direction = (
        next_direction(residual, coef, (high_ref[...], mid_ref[...], low_ref[...]))
        + beta * direction
    )
    for i in range(new_dir.shape[0]):
        new_res[i] = residual[:, i * BLOCK:(i + 1) * BLOCK]
        new_dir[i] = direction[:, i * BLOCK:(i + 1) * BLOCK]
        new_sol[i] = solution[:, i * BLOCK:(i + 1) * BLOCK]
    product(direction, key_ref, row_ref, out_ref)


def call(body, name, outs, scratch, *args):
    return pl.pallas_call(
        body,
        out_shape=[jax.ShapeDtypeStruct(shape, dtype) for shape, dtype in outs],
        scratch_shapes=scratch,
        compiler_params=pltpu.CompilerParams(vmem_limit_bytes=48 << 20),
        interpret=INTERPRET,
        name=name,
    )(*args)


def per_device(points, targets, pivots):
    own = points.shape[0]
    columns = targets.shape[1]
    u_size, chips = lax.axis_size(U), lax.axis_size(CHIPS)
    u_at, core = lax.axis_index(U), lax.axis_index("c")
    v_size = 2 * chips
    flat_pivots = pivots.reshape(-1)
    piv = flat_pivots.shape[0]
    part = piv // v_size
    per = columns // v_size

    packed = share(jnp.concatenate([points] + three_parts(targets.T), axis=0), U)
    key_points = packed[:, :own].reshape(u_size * own, -1)
    parts = packed[:, own:].astype(F32).reshape(u_size, 3, columns, own)
    residual = parts[:, 0] + parts[:, 1] + parts[:, 2]

    place = jnp.zeros((), jnp.int32)
    for axis in ALL:
        here = jnp.arange(u_size, dtype=jnp.int32) if axis in U else lax.axis_index(axis)
        place = place * lax.axis_size(axis) + here
    key_ids = (place[:, None] * own + jnp.arange(own, dtype=jnp.int32)[None, :]).reshape(1, -1)

    owned = (flat_pivots[:, None] == key_ids).astype(BF16)
    held = jnp.dot(owned, key_points, preferred_element_type=F32).astype(BF16)
    held = half(held, core) + partner(half(held, 1 - core))
    packed = swap(
        jnp.concatenate(
            [
                jnp.broadcast_to(points[None], (chips,) + points.shape),
                held.reshape(chips, part, -1),
            ],
            axis=1,
        ),
        CHIPS,
    )
    picked = jnp.sum(packed[:, own:].astype(F32), axis=0).astype(BF16)
    picked = share(picked, CHIPS)
    picked = core_first(picked, partner(picked)).reshape(piv, -1)
    row_points = packed[:, :own].reshape(chips * own, -1)
    row_points = jnp.concatenate([row_points, partner(row_points)], axis=0)

    piv_left, piv_right = augment(picked)
    key_left, _ = augment(key_points)
    _, row_right = augment(row_points)

    keys = u_size * own
    wide_shape = ((keys, piv), BF16)
    height = part + 8 * ((2 * per + 7) // 8)
    *wide, packed = call(
        setup_body, "setup_factor", [wide_shape] * 3 + [((v_size, height, piv), F32)],
        [pltpu.VMEM((piv, piv), F32)], piv_left, piv_right, key_left, residual,
    )
    factor = lax.dynamic_slice_in_dim(wide[0], u_at * own, own, 0)
    packed = jnp.sum(swap(half(packed, core) + partner(half(packed, 1 - core)), CHIPS), axis=0)
    packed = share(packed, CHIPS)
    packed = core_first(packed, partner(packed))

    state = ((u_size, columns, own), F32)
    scalar = ((columns, BLOCK), F32)
    partial_shape = ((v_size, columns, own), F32)
    inverse, projection, direction, inner, squares, partial = call(
        begin_body, "begin",
        [((piv, piv), F32), ((columns, piv), F32), state, scalar, scalar, partial_shape],
        [pltpu.VMEM((piv, piv), F32)], packed, residual, *wide, key_left, row_right,
    )
    solution_now = jnp.zeros(state[0], F32)
    for step in range(ITERS):
        direction_own = lax.dynamic_index_in_dim(direction, u_at, 0, keepdims=False)
        blocks = partial[:chips] + partner(partial[chips:])
        image_own = jnp.sum(swap(blocks, CHIPS), axis=0) + NOISE * direction_own
        if step + 1 == ITERS:
            break
        image = share(image_own, U)
        packed = call(
            project_body, "project", [((columns, piv + BLOCK), F32)], [],
            image, residual, direction, *wide,
        )[0]
        packed = share(packed + partner(packed), CHIPS)
        residual, direction, solution_now, projection, inner, squares, partial = call(
            advance_body, "advance",
            [state, state, state, ((columns, piv), F32), scalar, scalar, partial_shape], [],
            packed, image, residual, direction, solution_now, projection, inner, squares,
            inverse, *wide, key_left, row_right,
        )
    curve = jnp.sum(direction_own * image_own, axis=1)
    curve = jnp.zeros((1, BLOCK), F32).at[0, :columns].set(curve)
    curve = jnp.sum(share(curve, ALL), axis=0)
    alpha = inner[:, :1] / curve[0, :columns, None]
    solution_own = lax.dynamic_index_in_dim(solution_now, u_at, 0, keepdims=False)
    residual_own = lax.dynamic_index_in_dim(residual, u_at, 0, keepdims=False)
    solution_own = solution_own + alpha * direction_own
    residual_own = residual_own - alpha * image_own
    return (factor, solution_own.T, residual_own.T)


def solution(mesh):
    sizes = (4, 8, 2, 2, 2) if mesh.devices.size == 256 else (2, 2, 1, 2, 2)
    grid = Mesh(mesh.devices.reshape(sizes), ALL)
    return jax.shard_map(
        per_device,
        mesh=grid,
        in_specs=(P(ALL, None), P(ALL, None), P()),
        out_specs=(P(ALL, None), P(ALL, None), P(ALL, None)),
        check_vma=False,
    )
```

```python
import functools

import jax
import jax.numpy as jnp
from jax import lax
from jax.experimental import pallas as pl
from jax.experimental.pallas import tpu as pltpu
from jax.sharding import Mesh, PartitionSpec as P

ITERS = 3
NOISE = 0.5
JITTER = 0.05
HIGHEST = lax.Precision.HIGHEST
INTERPRET = False
GROUP = 8
STRIDE = 8
BLOCK = 128
F32 = jnp.float32
BF16 = jnp.bfloat16

U = ("z",)
CHIPS = ("x", "yh", "yl")
ALL = ("x", "z", "yh", "yl", "c")


def swap(blocks, axes):
    return lax.all_to_all(blocks, axes, 0, 0, tiled=False)


def share(block, axes):
    count = lax.axis_size(axes)
    return swap(jnp.broadcast_to(block[None], (count,) + block.shape), axes)


def partner(values):
    return lax.ppermute(values, "c", [(0, 1), (1, 0)])


def core_first(mine, other):
    first = lax.axis_index("c") == 0
    return jnp.concatenate([jnp.where(first, mine, other), jnp.where(first, other, mine)], axis=0)


def half(values, at):
    count = values.shape[0] // 2
    return lax.dynamic_slice_in_dim(values, at * count, count, 0)


def three_parts(values):
    high = lax.reduce_precision(values, 8, 7)
    rest = values - high
    middle = lax.reduce_precision(rest, 8, 7)
    low = rest - middle
    return [part.astype(BF16) for part in (high, middle, low)]


def dot_nt(left, right, precision=None):
    return lax.dot_general(
        left, right, (((1,), (1,)), ((), ())), precision=precision, preferred_element_type=F32
    )


def dot_nn(left, right, precision=None):
    return lax.dot_general(
        left, right, (((1,), (0,)), ((), ())), precision=precision, preferred_element_type=F32
    )


def split(values):
    high = values.astype(BF16)
    rest = values - high.astype(F32)
    middle = rest.astype(BF16)
    return high, middle, (rest - middle.astype(F32)).astype(BF16)


def extended(rows, left):
    wide = rows.astype(F32)
    lane = lax.broadcasted_iota(jnp.int32, wide.shape, 1)
    parts = split(jnp.sum(wide * wide, axis=1, keepdims=True) * (-1.0 / 64.0))
    first, ones = (0, 3) if left else (3, 0)
    tail = jnp.where((lane >= ones) & (lane < ones + 3), 1.0, 0.0)
    for k in range(3):
        tail = jnp.where(lane == first + k, parts[k].astype(F32), tail)
    head = (wide * 0.03125).astype(BF16) if left else rows
    return jnp.concatenate([head, tail.astype(BF16)], axis=1)


def stacked_dot(dot, values, wide):
    count = values.shape[0]
    parts = jnp.concatenate(split(values), axis=0)
    a = dot(parts, wide[0])
    b = dot(parts[:2 * count], wide[1])
    c = dot(parts[:count], wide[2])
    return a[:count] + ((a[count:2 * count] + b[:count]) + (a[2 * count:] + b[count:] + c))


def eliminate(groups):
    order = len(groups) * GROUP
    lane = lax.broadcasted_iota(jnp.int32, (GROUP, order), 1)
    sub = lax.broadcasted_iota(jnp.int32, (GROUP, order), 0)
    groups = list(groups)
    for first in range(0, order, STRIDE):
        at = first // GROUP
        cols = [None] * len(groups)
        for g in range(at, len(groups)):
            cols[g] = [
                jnp.broadcast_to(groups[g][:, first + j:first + j + 1], (GROUP, order))
                for j in range(STRIDE)
            ]
        home = groups[at]
        own = cols[at]
        rows, inverses, steps = [], [], []
        for j in range(STRIDE):
            r = first % GROUP + j
            inverse = 1.0 / jnp.broadcast_to(own[j][r:r + 1, :], (GROUP, order))
            mult = jnp.where(sub > r, own[j] * inverse, 0.0)
            steps.append(
                [
                    jnp.broadcast_to(own[l][r:r + 1, :], (GROUP, order))
                    for l in range(j + 1, STRIDE)
                ]
            )
            for l in range(j + 1, STRIDE):
                own[l] = own[l] - mult * steps[j][l - j - 1]
            row = jnp.where(
                lane == first + j, 1.0, jnp.broadcast_to(home[r:r + 1, :], (GROUP, order))
            )
            home = jnp.where((lane == first + j) & (sub > r), 0.0, home) - mult * row
            rows.append(jnp.where((lane > first + j) & (lane < first + STRIDE), 0.0, row))
            inverses.append(inverse)
        groups[at] = home
        for g in range(at + 1, len(groups)):
            col = cols[g]
            value = jnp.where((lane >= first) & (lane < first + STRIDE), 0.0, groups[g])
            for j in range(STRIDE):
                mult = col[j] * inverses[j]
                for l in range(j + 1, STRIDE):
                    col[l] = col[l] - mult * steps[j][l - j - 1]
                value = value - mult * rows[j]
            groups[g] = value
    return groups


def inverse_of_block(diag):
    if INTERPRET:
        return jnp.linalg.inv(jnp.linalg.cholesky(diag))
    groups = eliminate([diag[g:g + GROUP, :] for g in range(0, BLOCK, GROUP)])
    done = jnp.concatenate(groups, axis=0)
    row = lax.broadcasted_iota(jnp.int32, (BLOCK, BLOCK), 0)
    col = lax.broadcasted_iota(jnp.int32, (BLOCK, BLOCK), 1)
    pivots = jnp.sum(jnp.where(row == col, done, 0.0), axis=1, keepdims=True)
    unit = jnp.where(col < row, done, jnp.where(col == row, 1.0, 0.0))
    return unit * lax.rsqrt(pivots)


def inverse_factor(work_ref):
    order = work_ref.shape[0]

    def stage(j, carry):
        start = pl.multiple_of(j * BLOCK, BLOCK)
        here = pl.ds(start, BLOCK)
        below = lax.broadcasted_iota(jnp.int32, (order, BLOCK), 0) >= start + BLOCK
        local = inverse_of_block(work_ref[here, here])
        work_ref[here, :] = dot_nn(local, work_ref[here, :], HIGHEST)
        low = jnp.where(below, dot_nt(work_ref[:, here], local, HIGHEST), 0.0)
        work_ref[here, here] = local
        strip = work_ref[here, :]
        work_ref[:, here] = jnp.where(below, 0.0, work_ref[:, here])
        work_ref[...] = work_ref[...] - dot_nn(low, strip, HIGHEST)
        return carry

    lax.fori_loop(0, order // BLOCK, stage, 0)
    row = lax.broadcasted_iota(jnp.int32, (order, order), 0)
    col = lax.broadcasted_iota(jnp.int32, (order, order), 1)
    return jnp.where(col <= row, work_ref[...], 0.0)


def unit_matrix(order, scale):
    row = lax.broadcasted_iota(jnp.int32, (order, order), 0)
    col = lax.broadcasted_iota(jnp.int32, (order, order), 1)
    return jnp.where(row == col, scale, 0.0)


def joined(ref):
    return jnp.concatenate([ref[i] for i in range(ref.shape[0])], axis=1)


def setup_body(
    picked_ref, keys_ref, rows_ref, targets_ref,
    high_ref, mid_ref, low_ref, key_ref, row_ref, out_ref, work_ref, pack_ref,
):
    piv = picked_ref.shape[0]
    chunks = out_ref.shape[0]
    picked = picked_ref[...]
    right = extended(picked, False)
    work_ref[...] = jnp.exp(dot_nt(extended(picked, True), right)) + unit_matrix(piv, JITTER)
    key_ref[...] = extended(keys_ref[...], True)

    def rows_step(i, carry):
        here = pl.ds(pl.multiple_of(i * 256, 256), 256)
        row_ref[here, :] = extended(rows_ref[here, :], False)
        return carry

    lax.fori_loop(0, rows_ref.shape[0] // 256, rows_step, 0)
    inverse = inverse_factor(work_ref)
    wide = dot_nt(jnp.exp(dot_nt(key_ref[...], right)), inverse, HIGHEST)
    parts = split(wide)
    high_ref[...] = parts[0]
    mid_ref[...] = parts[1]
    low_ref[...] = parts[2]
    at = 0
    for i in range(piv // BLOCK):
        strip = lax.dot_general(
            wide[:, i * BLOCK:(i + 1) * BLOCK], wide[:, :(i + 1) * BLOCK],
            (((0,), (0,)), ((), ())), precision=HIGHEST, preferred_element_type=F32,
        )
        for j in range(i + 1):
            pack_ref[at:at + BLOCK, :] = strip[:, j * BLOCK:(j + 1) * BLOCK]
            at += BLOCK
    targets = joined(targets_ref)
    proj = dot_nn(targets, wide, HIGHEST)
    squares = jnp.broadcast_to(
        jnp.sum(targets * targets, axis=1, keepdims=True), (proj.shape[0], BLOCK)
    )
    part = at // chunks
    per = proj.shape[0] // chunks
    split_by = piv // BLOCK
    for i in range(chunks):
        out_ref[i, 0:part, :] = pack_ref[i * part:(i + 1) * part, :]
        for p in range(per):
            row = i * per + p
            for k in range(split_by):
                out_ref[i, part + p * split_by + k, :] = proj[row, k * BLOCK:(k + 1) * BLOCK]
            out_ref[i, part + per * split_by + p, :] = squares[row, :]


def gram_solve(proj, inverse):
    return stacked_dot(dot_nn, stacked_dot(dot_nt, proj, inverse), inverse)


def product(direction, key_ref, row_ref, out_ref):
    keys = key_ref.shape[0]
    count = direction.shape[0]
    parts = jnp.concatenate(split(direction), axis=0)
    chunk = 256

    def rows_step(i, carry):
        rows = row_ref[pl.ds(pl.multiple_of(i * chunk, chunk), chunk), :]
        total = jnp.zeros((count, chunk), F32)
        for start in range(0, keys, chunk):
            values = jnp.exp(dot_nt(key_ref[start:start + chunk, :], rows))
            high = values.astype(BF16)
            low = (values - high.astype(F32)).astype(BF16)
            a = dot_nn(parts[:, start:start + chunk], high)
            b = dot_nn(parts[:2 * count, start:start + chunk], low)
            total = total + (
                a[:count] + ((a[count:2 * count] + b[:count]) + (a[2 * count:] + b[count:]))
            )
        for k in range(chunk // BLOCK):
            out_ref[i * (chunk // BLOCK) + k] = total[:, k * BLOCK:(k + 1) * BLOCK]
        return carry

    lax.fori_loop(0, row_ref.shape[0] // chunk, rows_step, 0)


def next_direction(residual, coef, wide):
    return (residual - stacked_dot(dot_nt, coef, wide)) * (1.0 / NOISE)


def begin_body(
    packed_ref, res_ref, high_ref, mid_ref, low_ref, key_ref, row_ref,
    inv_high, inv_mid, inv_low, proj_ref, dir_ref, inner_ref, sq_ref, out_ref, work_ref, pack_ref,
):
    piv = work_ref.shape[0]
    chunks = packed_ref.shape[0]
    split_by = piv // BLOCK
    part = split_by * (split_by + 1) // 2 * BLOCK // chunks
    per = proj_ref.shape[0] // chunks
    for i in range(chunks):
        pack_ref[i * part:(i + 1) * part, :] = packed_ref[i, 0:part, :]
        for p in range(per):
            row = i * per + p
            for k in range(split_by):
                proj_ref[row, k * BLOCK:(k + 1) * BLOCK] = packed_ref[i, part + p * split_by + k, :]
            sq_ref[row, :] = packed_ref[i, part + per * split_by + p, :]
    at = 0
    for i in range(split_by):
        for j in range(i + 1):
            piece = pack_ref[at:at + BLOCK, :]
            work_ref[i * BLOCK:(i + 1) * BLOCK, j * BLOCK:(j + 1) * BLOCK] = piece
            if j < i:
                work_ref[j * BLOCK:(j + 1) * BLOCK, i * BLOCK:(i + 1) * BLOCK] = piece.T
            at += BLOCK
    work_ref[...] = work_ref[...] + unit_matrix(piv, NOISE)
    inverse = inverse_factor(work_ref)
    inverse = split(inverse)
    inv_high[...] = inverse[0]
    inv_mid[...] = inverse[1]
    inv_low[...] = inverse[2]
    proj = proj_ref[...]
    coef = gram_solve(proj, inverse)
    inner_ref[...] = (sq_ref[...] - jnp.sum(proj * coef, axis=1, keepdims=True)) * (1.0 / NOISE)
    direction = next_direction(joined(res_ref), coef, (high_ref[...], mid_ref[...], low_ref[...]))
    for i in range(dir_ref.shape[0]):
        dir_ref[i] = direction[:, i * BLOCK:(i + 1) * BLOCK]
    product(direction, key_ref, row_ref, out_ref)


def project_body(image_ref, res_ref, dir_ref, high_ref, mid_ref, low_ref, out_ref):
    image = joined(image_ref)
    residual = joined(res_ref)
    direction = joined(dir_ref)
    piv = high_ref.shape[1]
    out_ref[:, :piv] = stacked_dot(dot_nn, image, (high_ref[...], mid_ref[...], low_ref[...]))
    curve = jnp.sum(direction * image, axis=1, keepdims=True)
    cross = jnp.sum(residual * image, axis=1, keepdims=True)
    own = jnp.sum(image * image, axis=1, keepdims=True)
    lane = lax.broadcasted_iota(jnp.int32, (image.shape[0], BLOCK), 1)
    out_ref[:, piv:] = jnp.where(lane == 0, curve, jnp.where(lane == 1, cross, own))


def advance_body(
    packed_ref, image_ref, res_ref, dir_ref, sol_ref, proj_ref, inner_ref, sq_ref,
    inv_high, inv_mid, inv_low, high_ref, mid_ref, low_ref, key_ref, row_ref,
    new_res, new_dir, new_sol, new_proj, new_inner, new_sq, out_ref,
):
    piv = proj_ref.shape[1]
    total = packed_ref[0]
    for i in range(1, packed_ref.shape[0]):
        total = total + packed_ref[i]
    inner = inner_ref[:, 0:1]
    alpha = inner / total[:, piv:piv + 1]
    squares = (
        sq_ref[:, 0:1] - 2.0 * alpha * total[:, piv + 1:piv + 2]
        + alpha * alpha * total[:, piv + 2:piv + 3]
    )
    proj = proj_ref[...] - alpha * total[:, :piv]
    coef = gram_solve(proj, (inv_high[...], inv_mid[...], inv_low[...]))
    inner_next = (squares - jnp.sum(proj * coef, axis=1, keepdims=True)) * (1.0 / NOISE)
    beta = inner_next / inner
    new_proj[...] = proj
    new_inner[...] = jnp.broadcast_to(inner_next, new_inner.shape)
    new_sq[...] = jnp.broadcast_to(squares, new_sq.shape)
    direction = joined(dir_ref)
    residual = joined(res_ref) - alpha * joined(image_ref)
    solution = joined(sol_ref) + alpha * direction
    direction = (
        next_direction(residual, coef, (high_ref[...], mid_ref[...], low_ref[...]))
        + beta * direction
    )
    for i in range(new_dir.shape[0]):
        new_res[i] = residual[:, i * BLOCK:(i + 1) * BLOCK]
        new_dir[i] = direction[:, i * BLOCK:(i + 1) * BLOCK]
        new_sol[i] = solution[:, i * BLOCK:(i + 1) * BLOCK]
    product(direction, key_ref, row_ref, out_ref)


def call(body, name, outs, scratch, *args):
    return pl.pallas_call(
        body,
        out_shape=[jax.ShapeDtypeStruct(shape, dtype) for shape, dtype in outs],
        scratch_shapes=scratch,
        compiler_params=pltpu.CompilerParams(vmem_limit_bytes=48 << 20),
        interpret=INTERPRET,
        name=name,
    )(*args)


def per_device(points, targets, pivots):
    own = points.shape[0]
    columns = targets.shape[1]
    u_size, chips = lax.axis_size(U), lax.axis_size(CHIPS)
    u_at, core = lax.axis_index(U), lax.axis_index("c")
    v_size = 2 * chips
    flat_pivots = pivots.reshape(-1)
    piv = flat_pivots.shape[0]
    part = piv // v_size
    per = columns // v_size

    packed = share(jnp.concatenate([points] + three_parts(targets.T), axis=0), U)
    key_points = packed[:, :own].reshape(u_size * own, -1)
    parts = packed[:, own:].astype(F32).reshape(u_size, 3, columns, own)
    residual = parts[:, 0] + parts[:, 1] + parts[:, 2]

    place = jnp.zeros((), jnp.int32)
    for axis in ALL:
        here = jnp.arange(u_size, dtype=jnp.int32) if axis in U else lax.axis_index(axis)
        place = place * lax.axis_size(axis) + here
    key_ids = (place[:, None] * own + jnp.arange(own, dtype=jnp.int32)[None, :]).reshape(1, -1)

    owned = (flat_pivots[:, None] == key_ids).astype(BF16)
    held = jnp.dot(owned, key_points, preferred_element_type=F32).astype(BF16)
    held = half(held, core) + partner(half(held, 1 - core))
    packed = swap(
        jnp.concatenate(
            [
                jnp.broadcast_to(points[None], (chips,) + points.shape),
                held.reshape(chips, part, -1),
            ],
            axis=1,
        ),
        CHIPS,
    )
    picked = jnp.sum(packed[:, own:].astype(F32), axis=0).astype(BF16)
    picked = share(picked, CHIPS)
    picked = core_first(picked, partner(picked)).reshape(piv, -1)
    row_points = packed[:, :own].reshape(chips * own, -1)
    row_points = jnp.concatenate([row_points, partner(row_points)], axis=0)

    keys, rows = key_points.shape[0], row_points.shape[0]
    lower = piv // BLOCK * (piv // BLOCK + 1) // 2 * BLOCK
    height = (lower // v_size + per * (piv // BLOCK + 1) + 7) // 8 * 8
    work = [pltpu.VMEM((piv, piv), F32), pltpu.VMEM((lower, BLOCK), F32)]
    *wide, key_left, row_right, packed = call(
        setup_body, "setup_factor",
        [((keys, piv), BF16)] * 3
        + [((keys, 2 * BLOCK), BF16), ((rows, 2 * BLOCK), BF16), ((v_size, height, BLOCK), F32)],
        work, picked, key_points, row_points, residual,
    )
    factor = lax.dynamic_slice_in_dim(wide[0], u_at * own, own, 0)
    packed = jnp.sum(swap(half(packed, core) + partner(half(packed, 1 - core)), CHIPS), axis=0)
    packed = share(packed, CHIPS)
    packed = core_first(packed, partner(packed))

    state = ((u_size, columns, own), F32)
    scalar = ((columns, BLOCK), F32)
    partial_shape = ((v_size, columns, own), F32)
    *inverse, projection, direction, inner, squares, partial = call(
        begin_body, "begin",
        [((piv, piv), BF16)] * 3
        + [((columns, piv), F32), state, scalar, scalar, partial_shape],
        work, packed, residual, *wide, key_left, row_right,
    )
    solution_now = jnp.zeros(state[0], F32)
    for step in range(ITERS):
        direction_own = lax.dynamic_index_in_dim(direction, u_at, 0, keepdims=False)
        blocks = partial[:chips] + partner(partial[chips:])
        image_own = jnp.sum(swap(blocks, CHIPS), axis=0) + NOISE * direction_own
        if step + 1 == ITERS:
            break
        image = share(image_own, U)
        packed = call(
            project_body, "project", [((columns, piv + BLOCK), F32)], [],
            image, residual, direction, *wide,
        )[0]
        packed = packed + partner(packed)
        packed = packed + lax.ppermute(packed, CHIPS[2], [(0, 1), (1, 0)])
        packed = share(packed, CHIPS[:2])
        residual, direction, solution_now, projection, inner, squares, partial = call(
            advance_body, "advance",
            [state, state, state, ((columns, piv), F32), scalar, scalar, partial_shape], [],
            packed, image, residual, direction, solution_now, projection, inner, squares,
            *inverse, *wide, key_left, row_right,
        )
    curve = jnp.sum(direction_own * image_own, axis=1)
    curve = jnp.zeros((1, BLOCK), F32).at[0, :columns].set(curve)
    curve = jnp.sum(share(curve, ALL), axis=0)
    alpha = inner[:, :1] / curve[0, :columns, None]
    solution_own = lax.dynamic_index_in_dim(solution_now, u_at, 0, keepdims=False)
    residual_own = lax.dynamic_index_in_dim(residual, u_at, 0, keepdims=False)
    solution_own = solution_own + alpha * direction_own
    residual_own = residual_own - alpha * image_own
    return (factor, solution_own.T, residual_own.T)


def solution(mesh):
    sizes = (4, 8, 2, 2, 2) if mesh.devices.size == 256 else (2, 2, 1, 2, 2)
    grid = Mesh(mesh.devices.reshape(sizes), ALL)
    return jax.shard_map(
        per_device,
        mesh=grid,
        in_specs=(P(ALL, None), P(ALL, None), P()),
        out_specs=(P(ALL, None), P(ALL, None), P(ALL, None)),
        check_vma=False,
    )
```

```python
import functools

import jax
import jax.numpy as jnp
from jax import lax
from jax.experimental import pallas as pl
from jax.experimental.pallas import tpu as pltpu
from jax.sharding import Mesh, PartitionSpec as P

ITERS = 3
NOISE = 0.5
JITTER = 0.05
HIGHEST = lax.Precision.HIGHEST
INTERPRET = False
GROUP = 8
STRIDE = 8
BLOCK = 128
F32 = jnp.float32
BF16 = jnp.bfloat16

U = ("z",)
CHIPS = ("x", "yh", "yl")
ALL = ("x", "z", "yh", "yl", "c")


def swap(blocks, axes):
    return lax.all_to_all(blocks, axes, 0, 0, tiled=False)


def share(block, axes):
    count = lax.axis_size(axes)
    return swap(jnp.broadcast_to(block[None], (count,) + block.shape), axes)


def other_of_two(values, axis):
    count = lax.axis_size(axis)
    return lax.ppermute(values, axis, [(i, (i + 1) % count) for i in range(count)])


def partner(values):
    return other_of_two(values, "c")


def core_first(mine, other):
    first = lax.axis_index("c") == 0
    return jnp.concatenate([jnp.where(first, mine, other), jnp.where(first, other, mine)], axis=0)


def half(values, at):
    count = values.shape[0] // 2
    return lax.dynamic_slice_in_dim(values, at * count, count, 0)


def three_parts(values):
    high = lax.reduce_precision(values, 8, 7)
    rest = values - high
    middle = lax.reduce_precision(rest, 8, 7)
    low = rest - middle
    return [part.astype(BF16) for part in (high, middle, low)]


def dot_nt(left, right, precision=None):
    return lax.dot_general(
        left, right, (((1,), (1,)), ((), ())), precision=precision, preferred_element_type=F32
    )


def dot_nn(left, right, precision=None):
    return lax.dot_general(
        left, right, (((1,), (0,)), ((), ())), precision=precision, preferred_element_type=F32
    )


def dot_tn(left, right, precision=None):
    return lax.dot_general(
        left, right, (((0,), (0,)), ((), ())), precision=precision, preferred_element_type=F32
    )


def split(values):
    high = values.astype(BF16)
    rest = values - high.astype(F32)
    middle = rest.astype(BF16)
    return high, middle, (rest - middle.astype(F32)).astype(BF16)


def extended(rows, left):
    wide = rows.astype(F32)
    lane = lax.broadcasted_iota(jnp.int32, wide.shape, 1)
    parts = split(jnp.sum(wide * wide, axis=1, keepdims=True) * (-1.0 / 64.0))
    first, ones = (0, 3) if left else (3, 0)
    tail = jnp.where((lane >= ones) & (lane < ones + 3), 1.0, 0.0)
    for k in range(3):
        tail = jnp.where(lane == first + k, parts[k].astype(F32), tail)
    head = (wide * 0.03125).astype(BF16) if left else rows
    return jnp.concatenate([head, tail.astype(BF16)], axis=1)


def stacked_dot(dot, values, wide):
    count = values.shape[0]
    parts = jnp.concatenate(split(values), axis=0)
    a = dot(parts, wide[0])
    b = dot(parts[:2 * count], wide[1])
    c = dot(parts[:count], wide[2])
    return a[:count] + ((a[count:2 * count] + b[:count]) + (a[2 * count:] + b[count:] + c))


def eliminate(groups):
    order = len(groups) * GROUP
    lane = lax.broadcasted_iota(jnp.int32, (GROUP, order), 1)
    sub = lax.broadcasted_iota(jnp.int32, (GROUP, order), 0)
    groups = list(groups)
    for first in range(0, order, STRIDE):
        at = first // GROUP
        cols = [None] * len(groups)
        for g in range(at, len(groups)):
            cols[g] = [
                jnp.broadcast_to(groups[g][:, first + j:first + j + 1], (GROUP, order))
                for j in range(STRIDE)
            ]
        home = groups[at]
        own = cols[at]
        rows, inverses, steps = [], [], []
        for j in range(STRIDE):
            r = first % GROUP + j
            inverse = 1.0 / jnp.broadcast_to(own[j][r:r + 1, :], (GROUP, order))
            mult = jnp.where(sub > r, own[j] * inverse, 0.0)
            steps.append(
                [
                    jnp.broadcast_to(own[l][r:r + 1, :], (GROUP, order))
                    for l in range(j + 1, STRIDE)
                ]
            )
            for l in range(j + 1, STRIDE):
                own[l] = own[l] - mult * steps[j][l - j - 1]
            row = jnp.where(
                lane == first + j, 1.0, jnp.broadcast_to(home[r:r + 1, :], (GROUP, order))
            )
            home = jnp.where((lane == first + j) & (sub > r), 0.0, home) - mult * row
            rows.append(jnp.where((lane > first + j) & (lane < first + STRIDE), 0.0, row))
            inverses.append(inverse)
        groups[at] = home
        for g in range(at + 1, len(groups)):
            col = cols[g]
            value = jnp.where((lane >= first) & (lane < first + STRIDE), 0.0, groups[g])
            for j in range(STRIDE):
                mult = col[j] * inverses[j]
                for l in range(j + 1, STRIDE):
                    col[l] = col[l] - mult * steps[j][l - j - 1]
                value = value - mult * rows[j]
            groups[g] = value
    return groups


def inverse_of_block(diag):
    if INTERPRET:
        return jnp.linalg.inv(jnp.linalg.cholesky(diag))
    groups = eliminate([diag[g:g + GROUP, :] for g in range(0, BLOCK, GROUP)])
    done = jnp.concatenate(groups, axis=0)
    row = lax.broadcasted_iota(jnp.int32, (BLOCK, BLOCK), 0)
    col = lax.broadcasted_iota(jnp.int32, (BLOCK, BLOCK), 1)
    pivots = jnp.sum(jnp.where(row == col, done, 0.0), axis=1, keepdims=True)
    unit = jnp.where(col < row, done, jnp.where(col == row, 1.0, 0.0))
    return unit * lax.rsqrt(pivots)


def inverse_factor(work_ref):
    order = work_ref.shape[0]

    def stage(j, carry):
        start = pl.multiple_of(j * BLOCK, BLOCK)
        here = pl.ds(start, BLOCK)
        local = inverse_of_block(work_ref[here, here])
        strip = dot_nn(local, work_ref[here, :], HIGHEST)
        lane = lax.broadcasted_iota(jnp.int32, strip.shape, 1)
        upper = split(jnp.where(lane >= start + BLOCK, strip, 0.0))
        work_ref[here, :] = strip
        work_ref[here, here] = local
        strip = split(work_ref[here, :])
        below = lax.broadcasted_iota(jnp.int32, (order, BLOCK), 0) >= start + BLOCK
        work_ref[:, here] = jnp.where(below, 0.0, work_ref[:, here])
        high_mid = jnp.concatenate(upper[:2], axis=0)
        work_ref[...] = work_ref[...] - (
            dot_tn(high_mid, jnp.concatenate([strip[0], strip[0]], axis=0))
            + (
                dot_tn(high_mid, jnp.concatenate([strip[1], strip[1]], axis=0))
                + dot_tn(
                    jnp.concatenate([upper[0], upper[2]], axis=0),
                    jnp.concatenate([strip[2], strip[0]], axis=0),
                )
            )
        )
        return carry

    lax.fori_loop(0, order // BLOCK, stage, 0)
    row = lax.broadcasted_iota(jnp.int32, (order, order), 0)
    col = lax.broadcasted_iota(jnp.int32, (order, order), 1)
    return jnp.where(col <= row, work_ref[...], 0.0)


def unit_matrix(order, scale):
    row = lax.broadcasted_iota(jnp.int32, (order, order), 0)
    col = lax.broadcasted_iota(jnp.int32, (order, order), 1)
    return jnp.where(row == col, scale, 0.0)


def joined(ref):
    return jnp.concatenate([ref[i] for i in range(ref.shape[0])], axis=1)


def pivots_body(picked_ref, inv_ref, right_ref, work_ref):
    picked = picked_ref[...]
    right = extended(picked, False)
    right_ref[...] = right
    work_ref[...] = (
        jnp.exp(dot_nt(extended(picked, True), right)) + unit_matrix(picked.shape[0], JITTER)
    )
    inv_ref[...] = inverse_factor(work_ref)


def setup_body(
    inv_ref, right_ref, keys_ref, targets_ref,
    high_ref, mid_ref, low_ref, key_ref, out_ref, pack_ref,
):
    piv = inv_ref.shape[0]
    chunks = out_ref.shape[0]
    right = right_ref[...]
    inverse = inv_ref[...]
    key_ref[...] = extended(keys_ref[...], True)
    wide = dot_nt(jnp.exp(dot_nt(key_ref[...], right)), inverse, HIGHEST)
    parts = split(wide)
    high_ref[...] = parts[0]
    mid_ref[...] = parts[1]
    low_ref[...] = parts[2]
    at = 0
    for i in range(piv // BLOCK):
        strip = dot_tn(
            wide[:, i * BLOCK:(i + 1) * BLOCK], wide[:, :(i + 1) * BLOCK], HIGHEST
        )
        for j in range(i + 1):
            pack_ref[at:at + BLOCK, :] = strip[:, j * BLOCK:(j + 1) * BLOCK]
            at += BLOCK
    targets = joined(targets_ref)
    proj = dot_nn(targets, wide, HIGHEST)
    part = at // chunks
    per = proj.shape[0] // chunks
    split_by = piv // BLOCK
    for i in range(chunks):
        out_ref[i, 0:part, :] = pack_ref[i * part:(i + 1) * part, :]
        for p in range(per):
            row = i * per + p
            for k in range(split_by):
                out_ref[i, part + p * split_by + k, :] = proj[row, k * BLOCK:(k + 1) * BLOCK]


def gram_solve(proj, inverse):
    return stacked_dot(dot_nn, stacked_dot(dot_nt, proj, inverse), inverse)


def product(direction, key_ref, row_ref, out_ref):
    keys = key_ref.shape[0]
    count = direction.shape[0]
    parts = jnp.concatenate(split(direction), axis=0)
    chunk = 256

    for first in range(0, row_ref.shape[0], chunk):
        rows = row_ref[first:first + chunk, :]
        total = jnp.zeros((count, chunk), F32)
        for start in range(0, keys, chunk):
            values = jnp.exp(dot_nt(key_ref[start:start + chunk, :], rows))
            high = values.astype(BF16)
            low = (values - high.astype(F32)).astype(BF16)
            a = dot_nn(parts[:, start:start + chunk], high)
            b = dot_nn(parts[:2 * count, start:start + chunk], low)
            total = total + (
                a[:count] + ((a[count:2 * count] + b[:count]) + (a[2 * count:] + b[count:]))
            )
        for k in range(chunk // BLOCK):
            out_ref[first // BLOCK + k] = total[:, k * BLOCK:(k + 1) * BLOCK]


def next_direction(residual, coef, wide):
    return (residual - stacked_dot(dot_nt, coef, wide)) * (1.0 / NOISE)


def gram_body(packed_ref, inv_high, inv_mid, inv_low, proj_ref, work_ref, pack_ref):
    piv = work_ref.shape[0]
    chunks = packed_ref.shape[0]
    split_by = piv // BLOCK
    part = split_by * (split_by + 1) // 2 * BLOCK // chunks
    per = proj_ref.shape[0] // chunks
    for i in range(chunks):
        pack_ref[i * part:(i + 1) * part, :] = packed_ref[i, 0:part, :]
        for p in range(per):
            row = i * per + p
            for k in range(split_by):
                proj_ref[row, k * BLOCK:(k + 1) * BLOCK] = packed_ref[i, part + p * split_by + k, :]
    at = 0
    for i in range(split_by):
        for j in range(i + 1):
            piece = pack_ref[at:at + BLOCK, :]
            work_ref[i * BLOCK:(i + 1) * BLOCK, j * BLOCK:(j + 1) * BLOCK] = piece
            if j < i:
                work_ref[j * BLOCK:(j + 1) * BLOCK, i * BLOCK:(i + 1) * BLOCK] = piece.T
            at += BLOCK
    work_ref[...] = work_ref[...] + unit_matrix(piv, NOISE)
    inverse = inverse_factor(work_ref)
    inverse = split(inverse)
    inv_high[...] = inverse[0]
    inv_mid[...] = inverse[1]
    inv_low[...] = inverse[2]


def begin_body(
    proj_ref, inv_high, inv_mid, inv_low, res_ref, high_ref, mid_ref, low_ref, key_ref,
    points_ref, dir_ref, row_ref, out_ref,
):
    chips = points_ref.shape[0]
    for i in range(chips):
        for k in range(2):
            at = (k * chips + i) * BLOCK
            row_ref[at:at + BLOCK, :] = extended(points_ref[i, k * BLOCK:(k + 1) * BLOCK, :], False)
    coef = gram_solve(proj_ref[...], (inv_high[...], inv_mid[...], inv_low[...]))
    direction = next_direction(joined(res_ref), coef, (high_ref[...], mid_ref[...], low_ref[...]))
    for i in range(dir_ref.shape[0]):
        dir_ref[i] = direction[:, i * BLOCK:(i + 1) * BLOCK]
    product(direction, key_ref, row_ref, out_ref)


def project_body(image_ref, res_ref, dir_ref, high_ref, mid_ref, low_ref, out_ref):
    image = joined(image_ref)
    residual = joined(res_ref)
    direction = joined(dir_ref)
    piv = high_ref.shape[1]
    out_ref[:, :piv] = stacked_dot(dot_nn, image, (high_ref[...], mid_ref[...], low_ref[...]))
    curve = jnp.sum(direction * image, axis=1, keepdims=True)
    cross = jnp.sum(residual * image, axis=1, keepdims=True)
    own = jnp.sum(image * image, axis=1, keepdims=True)
    along = jnp.sum(direction * residual, axis=1, keepdims=True)
    squares = jnp.sum(residual * residual, axis=1, keepdims=True)
    lane = lax.broadcasted_iota(jnp.int32, (image.shape[0], BLOCK), 1)
    sums = jnp.where(lane == 0, curve, jnp.where(lane == 1, cross, own))
    out_ref[:, piv:] = jnp.where(lane == 3, along, jnp.where(lane == 4, squares, sums))


def advance_body(
    packed_ref, image_ref, res_ref, dir_ref, sol_ref, proj_ref,
    inv_high, inv_mid, inv_low, high_ref, mid_ref, low_ref, key_ref, row_ref,
    new_res, new_dir, new_sol, new_proj, out_ref,
):
    piv = proj_ref.shape[1]
    total = packed_ref[...]
    inner = total[:, piv + 3:piv + 4]
    alpha = inner / total[:, piv:piv + 1]
    squares = (
        total[:, piv + 4:piv + 5] - 2.0 * alpha * total[:, piv + 1:piv + 2]
        + alpha * alpha * total[:, piv + 2:piv + 3]
    )
    proj = proj_ref[...] - alpha * total[:, :piv]
    coef = gram_solve(proj, (inv_high[...], inv_mid[...], inv_low[...]))
    inner_next = (squares - jnp.sum(proj * coef, axis=1, keepdims=True)) * (1.0 / NOISE)
    beta = inner_next / inner
    new_proj[...] = proj
    direction = joined(dir_ref)
    residual = joined(res_ref) - alpha * joined(image_ref)
    solution = joined(sol_ref) + alpha * direction
    direction = (
        next_direction(residual, coef, (high_ref[...], mid_ref[...], low_ref[...]))
        + beta * direction
    )
    for i in range(new_dir.shape[0]):
        new_res[i] = residual[:, i * BLOCK:(i + 1) * BLOCK]
        new_dir[i] = direction[:, i * BLOCK:(i + 1) * BLOCK]
        new_sol[i] = solution[:, i * BLOCK:(i + 1) * BLOCK]
    product(direction, key_ref, row_ref, out_ref)


def call(body, name, outs, scratch, *args, seconds=10e-6):
    return pl.pallas_call(
        body,
        out_shape=[jax.ShapeDtypeStruct(shape, dtype) for shape, dtype in outs],
        scratch_shapes=scratch,
        compiler_params=pltpu.CompilerParams(vmem_limit_bytes=48 << 20),
        cost_estimate=pl.CostEstimate(
            flops=int(seconds * 1e15), bytes_accessed=int(seconds * 3e12), transcendentals=0
        ),
        interpret=INTERPRET,
        name=name,
    )(*args)


def per_device(points, targets, pivots):
    own = points.shape[0]
    columns = targets.shape[1]
    u_size, chips = lax.axis_size(U), lax.axis_size(CHIPS)
    u_at, core = lax.axis_index(U), lax.axis_index("c")
    v_size = 2 * chips
    flat_pivots = pivots.reshape(-1)
    piv = flat_pivots.shape[0]
    part = piv // v_size
    per = columns // v_size

    place = jnp.zeros((), jnp.int32)
    for axis in ALL:
        place = place * lax.axis_size(axis) + lax.axis_index(axis)
    own_ids = place * own + jnp.arange(own, dtype=jnp.int32)
    owned = (flat_pivots[:, None] == own_ids[None, :]).astype(BF16)
    held = jnp.dot(owned, points, preferred_element_type=F32).astype(BF16)
    held = half(held, core) + partner(half(held, 1 - core))
    picked = swap(held.reshape(chips, part, -1), CHIPS)
    picked = jnp.sum(picked.astype(F32), axis=0).astype(BF16)
    picked = jnp.sum(share(picked, U).astype(F32), axis=0).astype(BF16)
    picked = share(picked, CHIPS)
    picked = core_first(picked, partner(picked)).reshape(piv, -1)

    both_points = jnp.concatenate([points, partner(points)], axis=0)
    points, targets, picked = lax.optimization_barrier((points, targets, picked))
    packed = share(jnp.concatenate([points] + three_parts(targets.T), axis=0), U)
    key_points = packed[:, :own].reshape(u_size * own, -1)
    parts = packed[:, own:].astype(F32).reshape(u_size, 3, columns, own)
    residual = parts[:, 0] + parts[:, 1] + parts[:, 2]
    piv_inverse, piv_right = call(
        pivots_body, "pivots_factor", [((piv, piv), F32), ((piv, 2 * BLOCK), BF16)],
        [pltpu.VMEM((piv, piv), F32)], picked, seconds=22e-6,
    )

    keys = key_points.shape[0]
    lower = piv // BLOCK * (piv // BLOCK + 1) // 2 * BLOCK
    height = (lower // v_size + per * (piv // BLOCK) + 7) // 8 * 8
    work = [pltpu.VMEM((piv, piv), F32), pltpu.VMEM((lower, BLOCK), F32)]
    *wide, key_left, packed = call(
        setup_body, "setup_factor",
        [((keys, piv), BF16)] * 3
        + [((keys, 2 * BLOCK), BF16), ((v_size, height, BLOCK), F32)],
        work[1:], piv_inverse, piv_right, key_points, residual,
    )
    factor = lax.dynamic_slice_in_dim(wide[0], u_at * own, own, 0)
    packed = jnp.sum(swap(half(packed, core) + partner(half(packed, 1 - core)), CHIPS), axis=0)
    packed = share(packed, CHIPS)
    packed = core_first(packed, partner(packed))

    state = ((u_size, columns, own), F32)
    partial_shape = ((v_size, columns, own), F32)
    both_points, packed = lax.optimization_barrier((both_points, packed))
    row_points = share(both_points, CHIPS)
    *inverse, projection = call(
        gram_body, "gram_factor", [((piv, piv), BF16)] * 3 + [((columns, piv), F32)], work, packed,
        seconds=22e-6,
    )
    direction, row_right, partial = call(
        begin_body, "begin", [state, ((v_size * own, 2 * BLOCK), BF16), partial_shape], [],
        projection, *inverse, residual, *wide, key_left, row_points,
    )
    solution_now = jnp.zeros(state[0], F32)
    for step in range(ITERS):
        direction_own = lax.dynamic_index_in_dim(direction, u_at, 0, keepdims=False)
        blocks = partial[:chips] + partner(partial[chips:])
        image_own = jnp.sum(swap(blocks, CHIPS), axis=0) + NOISE * direction_own
        if step + 1 == ITERS:
            break
        image = share(image_own, U)
        packed = call(
            project_body, "project", [((columns, piv + BLOCK), F32)], [],
            image, residual, direction, *wide,
        )[0]
        packed = half(packed, core) + partner(half(packed, 1 - core))
        packed = packed + other_of_two(packed, CHIPS[1])
        packed = jnp.sum(share(packed, (CHIPS[0], CHIPS[2])), axis=0)
        packed = core_first(packed, partner(packed))
        residual, direction, solution_now, projection, partial = call(
            advance_body, "advance",
            [state, state, state, ((columns, piv), F32), partial_shape], [],
            packed, image, residual, direction, solution_now, projection,
            *inverse, *wide, key_left, row_right,
        )
    solution_own = lax.dynamic_index_in_dim(solution_now, u_at, 0, keepdims=False)
    residual_own = lax.dynamic_index_in_dim(residual, u_at, 0, keepdims=False)
    sums = jnp.concatenate(
        [
            jnp.sum(direction_own * image_own, axis=1),
            jnp.sum(direction_own * residual_own, axis=1),
            jnp.zeros((BLOCK - 2 * columns,), F32),
        ]
    )
    sums = jnp.sum(share(sums[None], ALL), axis=(0, 1))
    alpha = (sums[columns:2 * columns] / sums[:columns])[:, None]
    solution_own = solution_own + alpha * direction_own
    residual_own = residual_own - alpha * image_own
    return (factor, solution_own.T, residual_own.T)


def solution(mesh):
    sizes = (4, 8, 2, 2, 2) if mesh.devices.size == 256 else (1, 2, 2, 2, 2)
    grid = Mesh(mesh.devices.reshape(sizes), ALL)
    return jax.shard_map(
        per_device,
        mesh=grid,
        in_specs=(P(ALL, None), P(ALL, None), P()),
        out_specs=(P(ALL, None), P(ALL, None), P(ALL, None)),
        check_vma=False,
    )
```

```python
import functools

import jax
import jax.numpy as jnp
from jax import lax
from jax.experimental import pallas as pl
from jax.experimental.pallas import tpu as pltpu
from jax.sharding import Mesh, PartitionSpec as P

ITERS = 3
NOISE = 0.5
JITTER = 0.05
HIGHEST = lax.Precision.HIGHEST
INTERPRET = False
GROUP = 8
STRIDE = 8
BLOCK = 128
F32 = jnp.float32
BF16 = jnp.bfloat16

U = ("z",)
CHIPS = ("x", "yh", "yl")
ALL = ("x", "z", "yh", "yl", "c")


def swap(blocks, axes):
    return lax.all_to_all(blocks, axes, 0, 0, tiled=False)


def share(block, axes):
    count = lax.axis_size(axes)
    return swap(jnp.broadcast_to(block[None], (count,) + block.shape), axes)


def other_of_two(values, axis):
    count = lax.axis_size(axis)
    return lax.ppermute(values, axis, [(i, (i + 1) % count) for i in range(count)])


def partner(values):
    return other_of_two(values, "c")


def core_first(mine, other):
    first = lax.axis_index("c") == 0
    return jnp.concatenate([jnp.where(first, mine, other), jnp.where(first, other, mine)], axis=0)


def half(values, at):
    count = values.shape[0] // 2
    return lax.dynamic_slice_in_dim(values, at * count, count, 0)


def three_parts(values):
    high = lax.reduce_precision(values, 8, 7)
    rest = values - high
    middle = lax.reduce_precision(rest, 8, 7)
    low = rest - middle
    return [part.astype(BF16) for part in (high, middle, low)]


def dot_nt(left, right, precision=None):
    return lax.dot_general(
        left, right, (((1,), (1,)), ((), ())), precision=precision, preferred_element_type=F32
    )


def dot_nn(left, right, precision=None):
    return lax.dot_general(
        left, right, (((1,), (0,)), ((), ())), precision=precision, preferred_element_type=F32
    )


def dot_tn(left, right, precision=None):
    return lax.dot_general(
        left, right, (((0,), (0,)), ((), ())), precision=precision, preferred_element_type=F32
    )


def split(values):
    high = values.astype(BF16)
    rest = values - high.astype(F32)
    middle = rest.astype(BF16)
    return high, middle, (rest - middle.astype(F32)).astype(BF16)


def extended(rows, left):
    wide = rows.astype(F32)
    lane = lax.broadcasted_iota(jnp.int32, wide.shape, 1)
    parts = split(jnp.sum(wide * wide, axis=1, keepdims=True) * (-1.0 / 64.0))
    first, ones = (0, 3) if left else (3, 0)
    tail = jnp.where((lane >= ones) & (lane < ones + 3), 1.0, 0.0)
    for k in range(3):
        tail = jnp.where(lane == first + k, parts[k].astype(F32), tail)
    head = (wide * 0.03125).astype(BF16) if left else rows
    return jnp.concatenate([head, tail.astype(BF16)], axis=1)


def stacked_dot(dot, values, wide):
    count = values.shape[0]
    parts = jnp.concatenate(split(values), axis=0)
    a = dot(parts, wide[0])
    b = dot(parts[:2 * count], wide[1])
    c = dot(parts[:count], wide[2])
    return a[:count] + ((a[count:2 * count] + b[:count]) + (a[2 * count:] + b[count:] + c))


def eliminate(groups):
    order = len(groups) * GROUP
    lane = lax.broadcasted_iota(jnp.int32, (GROUP, order), 1)
    sub = lax.broadcasted_iota(jnp.int32, (GROUP, order), 0)
    groups = list(groups)
    for first in range(0, order, STRIDE):
        at = first // GROUP
        cols = [None] * len(groups)
        for g in range(at, len(groups)):
            cols[g] = [
                jnp.broadcast_to(groups[g][:, first + j:first + j + 1], (GROUP, order))
                for j in range(STRIDE)
            ]
        home = groups[at]
        own = cols[at]
        rows, inverses, steps = [], [], []
        for j in range(STRIDE):
            r = first % GROUP + j
            if j % 2 == 0:
                pivot = jnp.broadcast_to(own[j][r:r + 1, :], (GROUP, order))
                below = jnp.broadcast_to(own[j][r + 1:r + 2, :], (GROUP, order))
                beside = jnp.broadcast_to(own[j + 1][r:r + 1, :], (GROUP, order))
                corner = jnp.broadcast_to(own[j + 1][r + 1:r + 2, :], (GROUP, order))
                inverse = 1.0 / pivot
                following = pivot * (1.0 / (pivot * corner - below * beside))
            else:
                inverse = following
            mult = jnp.where(sub > r, own[j] * inverse, 0.0)
            steps.append(
                [
                    jnp.broadcast_to(own[l][r:r + 1, :], (GROUP, order))
                    for l in range(j + 1, STRIDE)
                ]
            )
            for l in range(j + 1, STRIDE):
                own[l] = own[l] - mult * steps[j][l - j - 1]
            row = jnp.where(
                lane == first + j, 1.0, jnp.broadcast_to(home[r:r + 1, :], (GROUP, order))
            )
            home = jnp.where((lane == first + j) & (sub > r), 0.0, home) - mult * row
            rows.append(jnp.where((lane > first + j) & (lane < first + STRIDE), 0.0, row))
            inverses.append(inverse)
        groups[at] = home
        for g in range(at + 1, len(groups)):
            col = cols[g]
            value = jnp.where((lane >= first) & (lane < first + STRIDE), 0.0, groups[g])
            for j in range(STRIDE):
                mult = col[j] * inverses[j]
                for l in range(j + 1, STRIDE):
                    col[l] = col[l] - mult * steps[j][l - j - 1]
                value = value - mult * rows[j]
            groups[g] = value
    return groups


def inverse_of_block(diag):
    if INTERPRET:
        return jnp.linalg.inv(jnp.linalg.cholesky(diag))
    groups = eliminate([diag[g:g + GROUP, :] for g in range(0, BLOCK, GROUP)])
    done = jnp.concatenate(groups, axis=0)
    row = lax.broadcasted_iota(jnp.int32, (BLOCK, BLOCK), 0)
    col = lax.broadcasted_iota(jnp.int32, (BLOCK, BLOCK), 1)
    pivots = jnp.sum(jnp.where(row == col, done, 0.0), axis=1, keepdims=True)
    unit = jnp.where(col < row, done, jnp.where(col == row, 1.0, 0.0))
    return unit * lax.rsqrt(pivots)


def inverse_factor(work_ref):
    order = work_ref.shape[0]

    def stage(j, carry):
        start = pl.multiple_of(j * BLOCK, BLOCK)
        here = pl.ds(start, BLOCK)
        local = inverse_of_block(work_ref[here, here])
        strip = dot_nn(local, work_ref[here, :], HIGHEST)
        lane = lax.broadcasted_iota(jnp.int32, strip.shape, 1)
        upper = split(jnp.where(lane >= start + BLOCK, strip, 0.0))
        work_ref[here, :] = strip
        work_ref[here, here] = local
        strip = split(work_ref[here, :])
        below = lax.broadcasted_iota(jnp.int32, (order, BLOCK), 0) >= start + BLOCK
        work_ref[:, here] = jnp.where(below, 0.0, work_ref[:, here])
        high_mid = jnp.concatenate(upper[:2], axis=0)
        work_ref[...] = work_ref[...] - (
            dot_tn(high_mid, jnp.concatenate([strip[0], strip[0]], axis=0))
            + (
                dot_tn(high_mid, jnp.concatenate([strip[1], strip[1]], axis=0))
                + dot_tn(
                    jnp.concatenate([upper[0], upper[2]], axis=0),
                    jnp.concatenate([strip[2], strip[0]], axis=0),
                )
            )
        )
        return carry

    lax.fori_loop(0, order // BLOCK, stage, 0)
    row = lax.broadcasted_iota(jnp.int32, (order, order), 0)
    col = lax.broadcasted_iota(jnp.int32, (order, order), 1)
    return jnp.where(col <= row, work_ref[...], 0.0)


def unit_matrix(order, scale):
    row = lax.broadcasted_iota(jnp.int32, (order, order), 0)
    col = lax.broadcasted_iota(jnp.int32, (order, order), 1)
    return jnp.where(row == col, scale, 0.0)


def joined(ref):
    return jnp.concatenate([ref[i] for i in range(ref.shape[0])], axis=1)


def pivots_body(picked_ref, inv_ref, right_ref, work_ref):
    picked = picked_ref[...]
    right = extended(picked, False)
    right_ref[...] = right
    work_ref[...] = (
        jnp.exp(dot_nt(extended(picked, True), right)) + unit_matrix(picked.shape[0], JITTER)
    )
    inv_ref[...] = inverse_factor(work_ref)


def setup_body(
    inv_ref, right_ref, keys_ref, targets_ref,
    high_ref, mid_ref, low_ref, key_ref, out_ref, pack_ref,
):
    piv = inv_ref.shape[0]
    chunks = out_ref.shape[0]
    right = right_ref[...]
    inverse = inv_ref[...]
    key_ref[...] = extended(keys_ref[...], True)
    wide = dot_nt(jnp.exp(dot_nt(key_ref[...], right)), inverse, HIGHEST)
    parts = split(wide)
    high_ref[...] = parts[0]
    mid_ref[...] = parts[1]
    low_ref[...] = parts[2]
    at = 0
    for i in range(piv // BLOCK):
        strip = dot_tn(
            wide[:, i * BLOCK:(i + 1) * BLOCK], wide[:, :(i + 1) * BLOCK], HIGHEST
        )
        for j in range(i + 1):
            pack_ref[at:at + BLOCK, :] = strip[:, j * BLOCK:(j + 1) * BLOCK]
            at += BLOCK
    targets = joined(targets_ref)
    proj = dot_nn(targets, wide, HIGHEST)
    part = at // chunks
    per = proj.shape[0] // chunks
    split_by = piv // BLOCK
    for i in range(chunks):
        out_ref[i, 0:part, :] = pack_ref[i * part:(i + 1) * part, :]
        for p in range(per):
            row = i * per + p
            for k in range(split_by):
                out_ref[i, part + p * split_by + k, :] = proj[row, k * BLOCK:(k + 1) * BLOCK]


def gram_solve(proj, inverse):
    return stacked_dot(dot_nn, stacked_dot(dot_nt, proj, inverse), inverse)


def product(direction, key_ref, row_ref, out_ref):
    keys = key_ref.shape[0]
    count = direction.shape[0]
    parts = jnp.concatenate(split(direction), axis=0)
    chunk = 256

    for first in range(0, row_ref.shape[0], chunk):
        rows = row_ref[first:first + chunk, :]
        total = jnp.zeros((count, chunk), F32)
        for start in range(0, keys, chunk):
            values = jnp.exp(dot_nt(key_ref[start:start + chunk, :], rows))
            high = values.astype(BF16)
            low = (values - high.astype(F32)).astype(BF16)
            a = dot_nn(parts[:, start:start + chunk], high)
            b = dot_nn(parts[:2 * count, start:start + chunk], low)
            total = total + (
                a[:count] + ((a[count:2 * count] + b[:count]) + (a[2 * count:] + b[count:]))
            )
        for k in range(chunk // BLOCK):
            out_ref[first // BLOCK + k] = total[:, k * BLOCK:(k + 1) * BLOCK]


def next_direction(residual, coef, wide):
    return (residual - stacked_dot(dot_nt, coef, wide)) * (1.0 / NOISE)


def gram_body(packed_ref, inv_high, inv_mid, inv_low, proj_ref, work_ref, pack_ref):
    piv = work_ref.shape[0]
    chunks = packed_ref.shape[0]
    split_by = piv // BLOCK
    part = split_by * (split_by + 1) // 2 * BLOCK // chunks
    per = proj_ref.shape[0] // chunks
    for i in range(chunks):
        pack_ref[i * part:(i + 1) * part, :] = packed_ref[i, 0:part, :]
        for p in range(per):
            row = i * per + p
            for k in range(split_by):
                proj_ref[row, k * BLOCK:(k + 1) * BLOCK] = packed_ref[i, part + p * split_by + k, :]
    at = 0
    for i in range(split_by):
        for j in range(i + 1):
            piece = pack_ref[at:at + BLOCK, :]
            work_ref[i * BLOCK:(i + 1) * BLOCK, j * BLOCK:(j + 1) * BLOCK] = piece
            if j < i:
                work_ref[j * BLOCK:(j + 1) * BLOCK, i * BLOCK:(i + 1) * BLOCK] = piece.T
            at += BLOCK
    work_ref[...] = work_ref[...] + unit_matrix(piv, NOISE)
    inverse = inverse_factor(work_ref)
    inverse = split(inverse)
    inv_high[...] = inverse[0]
    inv_mid[...] = inverse[1]
    inv_low[...] = inverse[2]


def begin_body(
    proj_ref, inv_high, inv_mid, inv_low, res_ref, high_ref, mid_ref, low_ref, key_ref,
    points_ref, dir_ref, row_ref, out_ref,
):
    chips = points_ref.shape[0]
    for i in range(chips):
        for k in range(2):
            at = (k * chips + i) * BLOCK
            row_ref[at:at + BLOCK, :] = extended(points_ref[i, k * BLOCK:(k + 1) * BLOCK, :], False)
    coef = gram_solve(proj_ref[...], (inv_high[...], inv_mid[...], inv_low[...]))
    direction = next_direction(joined(res_ref), coef, (high_ref[...], mid_ref[...], low_ref[...]))
    for i in range(dir_ref.shape[0]):
        dir_ref[i] = direction[:, i * BLOCK:(i + 1) * BLOCK]
    product(direction, key_ref, row_ref, out_ref)


def project_body(image_ref, res_ref, dir_ref, high_ref, mid_ref, low_ref, out_ref):
    image = joined(image_ref)
    residual = joined(res_ref)
    direction = joined(dir_ref)
    piv = high_ref.shape[1]
    out_ref[:, :piv] = stacked_dot(dot_nn, image, (high_ref[...], mid_ref[...], low_ref[...]))
    curve = jnp.sum(direction * image, axis=1, keepdims=True)
    cross = jnp.sum(residual * image, axis=1, keepdims=True)
    own = jnp.sum(image * image, axis=1, keepdims=True)
    along = jnp.sum(direction * residual, axis=1, keepdims=True)
    squares = jnp.sum(residual * residual, axis=1, keepdims=True)
    lane = lax.broadcasted_iota(jnp.int32, (image.shape[0], BLOCK), 1)
    sums = jnp.where(lane == 0, curve, jnp.where(lane == 1, cross, own))
    out_ref[:, piv:] = jnp.where(lane == 3, along, jnp.where(lane == 4, squares, sums))


def advance_body(
    packed_ref, image_ref, res_ref, dir_ref, sol_ref, proj_ref,
    inv_high, inv_mid, inv_low, high_ref, mid_ref, low_ref, key_ref, row_ref,
    new_res, new_dir, new_sol, new_proj, out_ref,
):
    piv = proj_ref.shape[1]
    total = packed_ref[...]
    inner = total[:, piv + 3:piv + 4]
    alpha = inner / total[:, piv:piv + 1]
    squares = (
        total[:, piv + 4:piv + 5] - 2.0 * alpha * total[:, piv + 1:piv + 2]
        + alpha * alpha * total[:, piv + 2:piv + 3]
    )
    proj = proj_ref[...] - alpha * total[:, :piv]
    coef = gram_solve(proj, (inv_high[...], inv_mid[...], inv_low[...]))
    inner_next = (squares - jnp.sum(proj * coef, axis=1, keepdims=True)) * (1.0 / NOISE)
    beta = inner_next / inner
    new_proj[...] = proj
    direction = joined(dir_ref)
    residual = joined(res_ref) - alpha * joined(image_ref)
    solution = joined(sol_ref) + alpha * direction
    direction = (
        next_direction(residual, coef, (high_ref[...], mid_ref[...], low_ref[...]))
        + beta * direction
    )
    for i in range(new_dir.shape[0]):
        new_res[i] = residual[:, i * BLOCK:(i + 1) * BLOCK]
        new_dir[i] = direction[:, i * BLOCK:(i + 1) * BLOCK]
        new_sol[i] = solution[:, i * BLOCK:(i + 1) * BLOCK]
    product(direction, key_ref, row_ref, out_ref)


def call(body, name, outs, scratch, *args, seconds=10e-6):
    spec = pl.BlockSpec(memory_space=pltpu.VMEM)
    return pl.pallas_call(
        body,
        in_specs=[spec] * len(args),
        out_specs=[spec] * len(outs),
        out_shape=[jax.ShapeDtypeStruct(shape, dtype) for shape, dtype in outs],
        scratch_shapes=scratch,
        compiler_params=pltpu.CompilerParams(vmem_limit_bytes=48 << 20),
        cost_estimate=pl.CostEstimate(
            flops=int(seconds * 1e15), bytes_accessed=int(seconds * 3e12), transcendentals=0
        ),
        interpret=INTERPRET,
        name=name,
    )(*args)


def per_device(points, targets, pivots):
    own = points.shape[0]
    columns = targets.shape[1]
    u_size, chips = lax.axis_size(U), lax.axis_size(CHIPS)
    u_at, core = lax.axis_index(U), lax.axis_index("c")
    v_size = 2 * chips
    flat_pivots = pivots.reshape(-1)
    piv = flat_pivots.shape[0]
    part = piv // v_size
    per = columns // v_size

    place = jnp.zeros((), jnp.int32)
    for axis in ALL:
        place = place * lax.axis_size(axis) + lax.axis_index(axis)
    own_ids = place * own + jnp.arange(own, dtype=jnp.int32)
    owned = (flat_pivots[:, None] == own_ids[None, :]).astype(BF16)
    held = jnp.dot(owned, points, preferred_element_type=F32).astype(BF16)
    held = half(held, core) + partner(half(held, 1 - core))
    picked = swap(held.reshape(chips, part, -1), CHIPS)
    picked = jnp.sum(picked.astype(F32), axis=0).astype(BF16)
    picked = jnp.sum(share(picked, U).astype(F32), axis=0).astype(BF16)
    picked = share(picked, CHIPS)
    picked = core_first(picked, partner(picked)).reshape(piv, -1)

    both_points = jnp.concatenate([points, partner(points)], axis=0)
    points, targets, picked = lax.optimization_barrier((points, targets, picked))
    packed = share(jnp.concatenate([points] + three_parts(targets.T), axis=0), U)
    key_points = packed[:, :own].reshape(u_size * own, -1)
    parts = packed[:, own:].astype(F32).reshape(u_size, 3, columns, own)
    residual = parts[:, 0] + parts[:, 1] + parts[:, 2]
    piv_inverse, piv_right = call(
        pivots_body, "pivots_factor", [((piv, piv), F32), ((piv, 2 * BLOCK), BF16)],
        [pltpu.VMEM((piv, piv), F32)], picked, seconds=22e-6,
    )

    keys = key_points.shape[0]
    lower = piv // BLOCK * (piv // BLOCK + 1) // 2 * BLOCK
    height = (lower // v_size + per * (piv // BLOCK) + 7) // 8 * 8
    work = [pltpu.VMEM((piv, piv), F32), pltpu.VMEM((lower, BLOCK), F32)]
    *wide, key_left, packed = call(
        setup_body, "setup_factor",
        [((keys, piv), BF16)] * 3
        + [((keys, 2 * BLOCK), BF16), ((v_size, height, BLOCK), F32)],
        work[1:], piv_inverse, piv_right, key_points, residual,
    )
    factor = lax.dynamic_slice_in_dim(wide[0], u_at * own, own, 0)
    packed = jnp.sum(swap(half(packed, core) + partner(half(packed, 1 - core)), CHIPS), axis=0)
    packed = share(packed, CHIPS)
    packed = core_first(packed, partner(packed))

    state = ((u_size, columns, own), F32)
    partial_shape = ((v_size, columns, own), F32)
    both_points, packed = lax.optimization_barrier((both_points, packed))
    row_points = share(both_points, CHIPS)
    *inverse, projection = call(
        gram_body, "gram_factor", [((piv, piv), BF16)] * 3 + [((columns, piv), F32)], work, packed,
        seconds=22e-6,
    )
    direction, row_right, partial = call(
        begin_body, "begin", [state, ((v_size * own, 2 * BLOCK), BF16), partial_shape], [],
        projection, *inverse, residual, *wide, key_left, row_points,
    )
    solution_now = jnp.zeros(state[0], F32)
    for step in range(ITERS):
        direction_own = lax.dynamic_index_in_dim(direction, u_at, 0, keepdims=False)
        blocks = partial[:chips] + partner(partial[chips:])
        image_own = jnp.sum(swap(blocks, CHIPS), axis=0) + NOISE * direction_own
        if step + 1 == ITERS:
            break
        image = share(image_own, U)
        packed = call(
            project_body, "project", [((columns, piv + BLOCK), F32)], [],
            image, residual, direction, *wide,
        )[0]
        packed = half(packed, core) + partner(half(packed, 1 - core))
        packed = jnp.sum(share(packed, CHIPS), axis=0)
        packed = core_first(packed, partner(packed))
        residual, direction, solution_now, projection, partial = call(
            advance_body, "advance",
            [state, state, state, ((columns, piv), F32), partial_shape], [],
            packed, image, residual, direction, solution_now, projection,
            *inverse, *wide, key_left, row_right,
        )
    solution_own = lax.dynamic_index_in_dim(solution_now, u_at, 0, keepdims=False)
    residual_own = lax.dynamic_index_in_dim(residual, u_at, 0, keepdims=False)
    sums = jnp.concatenate(
        [
            jnp.sum(direction_own * image_own, axis=1),
            jnp.sum(direction_own * residual_own, axis=1),
            jnp.zeros((BLOCK - 2 * columns,), F32),
        ]
    )
    sums = jnp.sum(share(sums[None], ALL), axis=(0, 1))
    alpha = (sums[columns:2 * columns] / sums[:columns])[:, None]
    solution_own = solution_own + alpha * direction_own
    residual_own = residual_own - alpha * image_own
    return (factor, solution_own.T, residual_own.T)


def solution(mesh):
    sizes = (4, 8, 2, 2, 2) if mesh.devices.size == 256 else (1, 2, 2, 2, 2)
    grid = Mesh(mesh.devices.reshape(sizes), ALL)
    return jax.shard_map(
        per_device,
        mesh=grid,
        in_specs=(P(ALL, None), P(ALL, None), P()),
        out_specs=(P(ALL, None), P(ALL, None), P(ALL, None)),
        check_vma=False,
    )
```

```python
import functools

import jax
import jax.numpy as jnp
from jax import lax
from jax.experimental import pallas as pl
from jax.experimental.pallas import tpu as pltpu
from jax.sharding import Mesh, PartitionSpec as P

ITERS = 3
NOISE = 0.5
JITTER = 0.05
HIGHEST = lax.Precision.HIGHEST
INTERPRET = False
GROUP = 8
STRIDE = 8
BLOCK = 128
F32 = jnp.float32
BF16 = jnp.bfloat16

U = ("z",)
CHIPS = ("x", "yh", "yl")
ALL = ("x", "z", "yh", "yl", "c")


def swap(blocks, axes):
    return lax.all_to_all(blocks, axes, 0, 0, tiled=False)


def share(block, axes):
    count = lax.axis_size(axes)
    return swap(jnp.broadcast_to(block[None], (count,) + block.shape), axes)


def other_of_two(values, axis):
    count = lax.axis_size(axis)
    return lax.ppermute(values, axis, [(i, (i + 1) % count) for i in range(count)])


def partner(values):
    return other_of_two(values, "c")


def core_first(mine, other):
    first = lax.axis_index("c") == 0
    return jnp.concatenate([jnp.where(first, mine, other), jnp.where(first, other, mine)], axis=0)


def half(values, at):
    count = values.shape[0] // 2
    return lax.dynamic_slice_in_dim(values, at * count, count, 0)


def three_parts(values):
    high = lax.reduce_precision(values, 8, 7)
    rest = values - high
    middle = lax.reduce_precision(rest, 8, 7)
    low = rest - middle
    return [part.astype(BF16) for part in (high, middle, low)]


def dot_nt(left, right, precision=None):
    return lax.dot_general(
        left, right, (((1,), (1,)), ((), ())), precision=precision, preferred_element_type=F32
    )


def dot_nn(left, right, precision=None):
    return lax.dot_general(
        left, right, (((1,), (0,)), ((), ())), precision=precision, preferred_element_type=F32
    )


def dot_tn(left, right, precision=None):
    return lax.dot_general(
        left, right, (((0,), (0,)), ((), ())), precision=precision, preferred_element_type=F32
    )


def split(values):
    high = values.astype(BF16)
    rest = values - high.astype(F32)
    middle = rest.astype(BF16)
    return high, middle, (rest - middle.astype(F32)).astype(BF16)


def extended(rows, left):
    wide = rows.astype(F32)
    lane = lax.broadcasted_iota(jnp.int32, wide.shape, 1)
    parts = split(jnp.sum(wide * wide, axis=1, keepdims=True) * (-1.0 / 64.0))
    first, ones = (0, 3) if left else (3, 0)
    tail = jnp.where((lane >= ones) & (lane < ones + 3), 1.0, 0.0)
    for k in range(3):
        tail = jnp.where(lane == first + k, parts[k].astype(F32), tail)
    head = (wide * 0.03125).astype(BF16) if left else rows
    return jnp.concatenate([head, tail.astype(BF16)], axis=1)


def stacked_dot(dot, values, wide):
    count = values.shape[0]
    parts = jnp.concatenate(split(values), axis=0)
    a = dot(parts, wide[0])
    b = dot(parts[:2 * count], wide[1])
    c = dot(parts[:count], wide[2])
    return a[:count] + ((a[count:2 * count] + b[:count]) + (a[2 * count:] + b[count:] + c))


def eliminate(groups):
    order = len(groups) * GROUP
    lane = lax.broadcasted_iota(jnp.int32, (GROUP, order), 1)
    sub = lax.broadcasted_iota(jnp.int32, (GROUP, order), 0)
    groups = list(groups)
    for first in range(0, order, STRIDE):
        at = first // GROUP
        cols = [None] * len(groups)
        for g in range(at, len(groups)):
            cols[g] = [
                jnp.broadcast_to(groups[g][:, first + j:first + j + 1], (GROUP, order))
                for j in range(STRIDE)
            ]
        home = groups[at]
        own = cols[at]
        rows, inverses, steps = [], [], []
        for j in range(STRIDE):
            r = first % GROUP + j
            inverse = 1.0 / jnp.broadcast_to(own[j][r:r + 1, :], (GROUP, order))
            mult = jnp.where(sub > r, own[j] * inverse, 0.0)
            steps.append(
                [
                    jnp.broadcast_to(own[l][r:r + 1, :], (GROUP, order))
                    for l in range(j + 1, STRIDE)
                ]
            )
            for l in range(j + 1, STRIDE):
                own[l] = own[l] - mult * steps[j][l - j - 1]
            row = jnp.where(
                lane == first + j, 1.0, jnp.broadcast_to(home[r:r + 1, :], (GROUP, order))
            )
            home = jnp.where((lane == first + j) & (sub > r), 0.0, home) - mult * row
            rows.append(jnp.where((lane > first + j) & (lane < first + STRIDE), 0.0, row))
            inverses.append(inverse)
        groups[at] = home
        for g in range(at + 1, len(groups)):
            col = cols[g]
            value = jnp.where((lane >= first) & (lane < first + STRIDE), 0.0, groups[g])
            for j in range(STRIDE):
                mult = col[j] * inverses[j]
                for l in range(j + 1, STRIDE):
                    col[l] = col[l] - mult * steps[j][l - j - 1]
                value = value - mult * rows[j]
            groups[g] = value
    return groups


def inverse_of_block(diag):
    if INTERPRET:
        return jnp.linalg.inv(jnp.linalg.cholesky(diag))
    groups = eliminate([diag[g:g + GROUP, :] for g in range(0, BLOCK, GROUP)])
    done = jnp.concatenate(groups, axis=0)
    row = lax.broadcasted_iota(jnp.int32, (BLOCK, BLOCK), 0)
    col = lax.broadcasted_iota(jnp.int32, (BLOCK, BLOCK), 1)
    pivots = jnp.sum(jnp.where(row == col, done, 0.0), axis=1, keepdims=True)
    unit = jnp.where(col < row, done, jnp.where(col == row, 1.0, 0.0))
    return unit * lax.rsqrt(pivots)


def inverse_factor(work_ref):
    order = work_ref.shape[0]

    def stage(j, carry):
        start = pl.multiple_of(j * BLOCK, BLOCK)
        here = pl.ds(start, BLOCK)
        local = inverse_of_block(work_ref[here, here])
        strip = dot_nn(local, work_ref[here, :], HIGHEST)
        lane = lax.broadcasted_iota(jnp.int32, strip.shape, 1)
        upper = split(jnp.where(lane >= start + BLOCK, strip, 0.0))
        work_ref[here, :] = strip
        work_ref[here, here] = local
        strip = split(work_ref[here, :])
        below = lax.broadcasted_iota(jnp.int32, (order, BLOCK), 0) >= start + BLOCK
        work_ref[:, here] = jnp.where(below, 0.0, work_ref[:, here])
        high_mid = jnp.concatenate(upper[:2], axis=0)
        work_ref[...] = work_ref[...] - (
            dot_tn(high_mid, jnp.concatenate([strip[0], strip[0]], axis=0))
            + (
                dot_tn(high_mid, jnp.concatenate([strip[1], strip[1]], axis=0))
                + dot_tn(
                    jnp.concatenate([upper[0], upper[2]], axis=0),
                    jnp.concatenate([strip[2], strip[0]], axis=0),
                )
            )
        )
        return carry

    lax.fori_loop(0, order // BLOCK, stage, 0)
    row = lax.broadcasted_iota(jnp.int32, (order, order), 0)
    col = lax.broadcasted_iota(jnp.int32, (order, order), 1)
    return jnp.where(col <= row, work_ref[...], 0.0)


def unit_matrix(order, scale):
    row = lax.broadcasted_iota(jnp.int32, (order, order), 0)
    col = lax.broadcasted_iota(jnp.int32, (order, order), 1)
    return jnp.where(row == col, scale, 0.0)


def joined(ref):
    return jnp.concatenate([ref[i] for i in range(ref.shape[0])], axis=1)


def pivots_body(picked_ref, inv_ref, work_ref):
    picked = picked_ref[...]
    right = extended(picked, False)
    work_ref[...] = (
        jnp.exp(dot_nt(extended(picked, True), right)) + unit_matrix(picked.shape[0], JITTER)
    )
    inv_ref[...] = inverse_factor(work_ref)


def setup_body(
    inv_ref, picked_ref, keys_ref, targets_ref,
    high_ref, mid_ref, low_ref, key_ref, out_ref, pack_ref,
):
    piv = inv_ref.shape[0]
    chunks = out_ref.shape[0]
    right = extended(picked_ref[...], False)
    inverse = inv_ref[...]
    key_ref[...] = extended(keys_ref[...], True)
    wide = dot_nt(jnp.exp(dot_nt(key_ref[...], right)), inverse, HIGHEST)
    parts = split(wide)
    high_ref[...] = parts[0]
    mid_ref[...] = parts[1]
    low_ref[...] = parts[2]
    at = 0
    for i in range(piv // BLOCK):
        strip = dot_tn(
            wide[:, i * BLOCK:(i + 1) * BLOCK], wide[:, :(i + 1) * BLOCK], HIGHEST
        )
        for j in range(i + 1):
            pack_ref[at:at + BLOCK, :] = strip[:, j * BLOCK:(j + 1) * BLOCK]
            at += BLOCK
    targets = joined(targets_ref)
    proj = dot_nn(targets, wide, HIGHEST)
    part = at // chunks
    per = proj.shape[0] // chunks
    split_by = piv // BLOCK
    for i in range(chunks):
        out_ref[i, 0:part, :] = pack_ref[i * part:(i + 1) * part, :]
        for p in range(per):
            row = i * per + p
            for k in range(split_by):
                out_ref[i, part + p * split_by + k, :] = proj[row, k * BLOCK:(k + 1) * BLOCK]


def gram_solve(proj, inverse):
    return stacked_dot(dot_nn, stacked_dot(dot_nt, proj, inverse), inverse)


def product(direction, key_ref, row_ref, out_ref):
    keys = key_ref.shape[0]
    count = direction.shape[0]
    parts = jnp.concatenate(split(direction), axis=0)
    chunk = 256

    for first in range(0, row_ref.shape[0], chunk):
        rows = row_ref[first:first + chunk, :]
        total = jnp.zeros((count, chunk), F32)
        for start in range(0, keys, chunk):
            values = jnp.exp(dot_nt(key_ref[start:start + chunk, :], rows))
            high = values.astype(BF16)
            low = (values - high.astype(F32)).astype(BF16)
            a = dot_nn(parts[:, start:start + chunk], high)
            b = dot_nn(parts[:2 * count, start:start + chunk], low)
            total = total + (
                a[:count] + ((a[count:2 * count] + b[:count]) + (a[2 * count:] + b[count:]))
            )
        for k in range(chunk // BLOCK):
            out_ref[first // BLOCK + k] = total[:, k * BLOCK:(k + 1) * BLOCK]


def next_direction(residual, coef, wide):
    return (residual - stacked_dot(dot_nt, coef, wide)) * (1.0 / NOISE)


def gram_body(packed_ref, inv_ref, proj_ref, work_ref, pack_ref):
    piv = work_ref.shape[0]
    chunks = packed_ref.shape[0]
    split_by = piv // BLOCK
    part = split_by * (split_by + 1) // 2 * BLOCK // chunks
    per = proj_ref.shape[0] // chunks
    for i in range(chunks):
        pack_ref[i * part:(i + 1) * part, :] = packed_ref[i, 0:part, :]
        for p in range(per):
            row = i * per + p
            for k in range(split_by):
                proj_ref[row, k * BLOCK:(k + 1) * BLOCK] = packed_ref[i, part + p * split_by + k, :]
    at = 0
    for i in range(split_by):
        for j in range(i + 1):
            piece = pack_ref[at:at + BLOCK, :]
            work_ref[i * BLOCK:(i + 1) * BLOCK, j * BLOCK:(j + 1) * BLOCK] = piece
            if j < i:
                work_ref[j * BLOCK:(j + 1) * BLOCK, i * BLOCK:(i + 1) * BLOCK] = piece.T
            at += BLOCK
    work_ref[...] = work_ref[...] + unit_matrix(piv, NOISE)
    inv_ref[...] = inverse_factor(work_ref)


def begin_body(
    proj_ref, inv_ref, res_ref, high_ref, mid_ref, low_ref, key_ref,
    points_ref, dir_ref, row_ref, out_ref,
):
    chips = points_ref.shape[0]
    for i in range(chips):
        for k in range(2):
            at = (k * chips + i) * BLOCK
            row_ref[at:at + BLOCK, :] = extended(points_ref[i, k * BLOCK:(k + 1) * BLOCK, :], False)
    coef = gram_solve(proj_ref[...], split(inv_ref[...]))
    direction = next_direction(joined(res_ref), coef, (high_ref[...], mid_ref[...], low_ref[...]))
    for i in range(dir_ref.shape[0]):
        dir_ref[i] = direction[:, i * BLOCK:(i + 1) * BLOCK]
    product(direction, key_ref, row_ref, out_ref)


def project_body(image_ref, res_ref, dir_ref, high_ref, mid_ref, low_ref, out_ref):
    image = joined(image_ref)
    residual = joined(res_ref)
    direction = joined(dir_ref)
    piv = high_ref.shape[1]
    out_ref[:, :piv] = stacked_dot(dot_nn, image, (high_ref[...], mid_ref[...], low_ref[...]))
    curve = jnp.sum(direction * image, axis=1, keepdims=True)
    cross = jnp.sum(residual * image, axis=1, keepdims=True)
    own = jnp.sum(image * image, axis=1, keepdims=True)
    along = jnp.sum(direction * residual, axis=1, keepdims=True)
    squares = jnp.sum(residual * residual, axis=1, keepdims=True)
    lane = lax.broadcasted_iota(jnp.int32, (image.shape[0], BLOCK), 1)
    sums = jnp.where(lane == 0, curve, jnp.where(lane == 1, cross, own))
    out_ref[:, piv:] = jnp.where(lane == 3, along, jnp.where(lane == 4, squares, sums))


def advance_body(
    packed_ref, image_ref, res_ref, dir_ref, sol_ref, proj_ref,
    inv_ref, high_ref, mid_ref, low_ref, key_ref, row_ref,
    new_res, new_dir, new_sol, new_proj, out_ref,
):
    piv = proj_ref.shape[1]
    total = packed_ref[...]
    inner = total[:, piv + 3:piv + 4]
    alpha = inner / total[:, piv:piv + 1]
    squares = (
        total[:, piv + 4:piv + 5] - 2.0 * alpha * total[:, piv + 1:piv + 2]
        + alpha * alpha * total[:, piv + 2:piv + 3]
    )
    proj = proj_ref[...] - alpha * total[:, :piv]
    coef = gram_solve(proj, split(inv_ref[...]))
    inner_next = (squares - jnp.sum(proj * coef, axis=1, keepdims=True)) * (1.0 / NOISE)
    beta = inner_next / inner
    new_proj[...] = proj
    direction = joined(dir_ref)
    residual = joined(res_ref) - alpha * joined(image_ref)
    solution = joined(sol_ref) + alpha * direction
    direction = (
        next_direction(residual, coef, (high_ref[...], mid_ref[...], low_ref[...]))
        + beta * direction
    )
    for i in range(new_dir.shape[0]):
        new_res[i] = residual[:, i * BLOCK:(i + 1) * BLOCK]
        new_dir[i] = direction[:, i * BLOCK:(i + 1) * BLOCK]
        new_sol[i] = solution[:, i * BLOCK:(i + 1) * BLOCK]
    product(direction, key_ref, row_ref, out_ref)


def call(body, name, outs, scratch, *args, seconds=10e-6):
    return pl.pallas_call(
        body,
        out_shape=[jax.ShapeDtypeStruct(shape, dtype) for shape, dtype in outs],
        scratch_shapes=scratch,
        compiler_params=pltpu.CompilerParams(vmem_limit_bytes=48 << 20),
        cost_estimate=pl.CostEstimate(
            flops=int(seconds * 1e15), bytes_accessed=int(seconds * 3e12), transcendentals=0
        ),
        interpret=INTERPRET,
        name=name,
    )(*args)


def per_device(points, targets, pivots):
    own = points.shape[0]
    columns = targets.shape[1]
    u_size, chips = lax.axis_size(U), lax.axis_size(CHIPS)
    u_at, core = lax.axis_index(U), lax.axis_index("c")
    v_size = 2 * chips
    flat_pivots = pivots.reshape(-1)
    piv = flat_pivots.shape[0]
    part = piv // v_size
    per = columns // v_size

    place = jnp.zeros((), jnp.int32)
    for axis in ALL:
        place = place * lax.axis_size(axis) + lax.axis_index(axis)
    own_ids = place * own + jnp.arange(own, dtype=jnp.int32)
    owned = (flat_pivots[:, None] == own_ids[None, :]).astype(BF16)
    held = jnp.dot(owned, points, preferred_element_type=F32).astype(BF16)
    total = u_size * v_size
    picked = swap(held.reshape(total, piv // total, -1), ALL)
    picked = jnp.sum(picked.astype(F32), axis=0).astype(BF16)
    picked = share(picked, ALL).reshape(piv, -1)

    both_points = jnp.concatenate([points, partner(points)], axis=0)
    points, targets, picked = lax.optimization_barrier((points, targets, picked))
    packed = share(jnp.concatenate([points] + three_parts(targets.T), axis=0), U)
    key_points = packed[:, :own].reshape(u_size * own, -1)
    parts = packed[:, own:].astype(F32).reshape(u_size, 3, columns, own)
    residual = parts[:, 0] + parts[:, 1] + parts[:, 2]
    piv_inverse = call(
        pivots_body, "pivots_factor", [((piv, piv), F32)], [pltpu.VMEM((piv, piv), F32)], picked,
        seconds=22e-6,
    )[0]

    keys = key_points.shape[0]
    lower = piv // BLOCK * (piv // BLOCK + 1) // 2 * BLOCK
    height = (lower // v_size + per * (piv // BLOCK) + 7) // 8 * 8
    work = [pltpu.VMEM((piv, piv), F32), pltpu.VMEM((lower, BLOCK), F32)]
    *wide, key_left, packed = call(
        setup_body, "setup_factor",
        [((keys, piv), BF16)] * 3
        + [((keys, 2 * BLOCK), BF16), ((v_size, height, BLOCK), F32)],
        work[1:], piv_inverse, picked, key_points, residual,
    )
    factor = lax.dynamic_slice_in_dim(wide[0], u_at * own, own, 0)
    packed = jnp.sum(swap(half(packed, core) + partner(half(packed, 1 - core)), CHIPS), axis=0)
    packed = share(packed, CHIPS)
    packed = core_first(packed, partner(packed))

    state = ((u_size, columns, own), F32)
    partial_shape = ((v_size, columns, own), F32)
    both_points, packed = lax.optimization_barrier((both_points, packed))
    row_points = share(both_points, CHIPS)
    inverse, projection = call(
        gram_body, "gram_factor", [((piv, piv), F32), ((columns, piv), F32)], work, packed,
        seconds=22e-6,
    )
    direction, row_right, partial = call(
        begin_body, "begin", [state, ((v_size * own, 2 * BLOCK), BF16), partial_shape], [],
        projection, inverse, residual, *wide, key_left, row_points,
    )
    solution_now = jnp.zeros(state[0], F32)
    for step in range(ITERS):
        direction_own = lax.dynamic_index_in_dim(direction, u_at, 0, keepdims=False)
        blocks = partial[:chips] + partner(partial[chips:])
        image_own = jnp.sum(swap(blocks, CHIPS), axis=0) + NOISE * direction_own
        if step + 1 == ITERS:
            break
        image = share(image_own, U)
        packed = call(
            project_body, "project", [((columns, piv + BLOCK), F32)], [],
            image, residual, direction, *wide,
        )[0]
        packed = half(packed, core) + partner(half(packed, 1 - core))
        packed = packed + other_of_two(packed, CHIPS[1])
        packed = jnp.sum(share(packed, (CHIPS[0], CHIPS[2])), axis=0)
        packed = core_first(packed, partner(packed))
        residual, direction, solution_now, projection, partial = call(
            advance_body, "advance",
            [state, state, state, ((columns, piv), F32), partial_shape], [],
            packed, image, residual, direction, solution_now, projection,
            inverse, *wide, key_left, row_right,
        )
    solution_own = lax.dynamic_index_in_dim(solution_now, u_at, 0, keepdims=False)
    residual_own = lax.dynamic_index_in_dim(residual, u_at, 0, keepdims=False)
    sums = jnp.concatenate(
        [
            jnp.sum(direction_own * image_own, axis=1),
            jnp.sum(direction_own * residual_own, axis=1),
            jnp.zeros((BLOCK - 2 * columns,), F32),
        ]
    )
    sums = jnp.sum(share(sums[None], ALL), axis=(0, 1))
    alpha = (sums[columns:2 * columns] / sums[:columns])[:, None]
    solution_own = solution_own + alpha * direction_own
    residual_own = residual_own - alpha * image_own
    return (factor, solution_own.T, residual_own.T)


def solution(mesh):
    sizes = (4, 8, 2, 2, 2) if mesh.devices.size == 256 else (1, 2, 2, 2, 2)
    grid = Mesh(mesh.devices.reshape(sizes), ALL)
    return jax.shard_map(
        per_device,
        mesh=grid,
        in_specs=(P(ALL, None), P(ALL, None), P()),
        out_specs=(P(ALL, None), P(ALL, None), P(ALL, None)),
        check_vma=False,
    )
```

```python
import functools

import jax
import jax.numpy as jnp
from jax import lax
from jax.experimental import pallas as pl
from jax.experimental.pallas import tpu as pltpu
from jax.sharding import Mesh, PartitionSpec as P

ITERS = 3
NOISE = 0.5
JITTER = 0.05
HIGHEST = lax.Precision.HIGHEST
INTERPRET = False
GROUP = 8
STRIDE = 8
BLOCK = 128
F32 = jnp.float32
BF16 = jnp.bfloat16

U = ("z",)
CHIPS = ("x", "yh", "yl")
ALL = ("x", "z", "yh", "yl", "c")


def swap(blocks, axes):
    return lax.all_to_all(blocks, axes, 0, 0, tiled=False)


def share(block, axes):
    count = lax.axis_size(axes)
    return swap(jnp.broadcast_to(block[None], (count,) + block.shape), axes)


def other_of_two(values, axis):
    count = lax.axis_size(axis)
    return lax.ppermute(values, axis, [(i, (i + 1) % count) for i in range(count)])


def partner(values):
    return other_of_two(values, "c")


def core_first(mine, other):
    first = lax.axis_index("c") == 0
    return jnp.concatenate([jnp.where(first, mine, other), jnp.where(first, other, mine)], axis=0)


def half(values, at):
    count = values.shape[0] // 2
    return lax.dynamic_slice_in_dim(values, at * count, count, 0)


def three_parts(values):
    high = lax.reduce_precision(values, 8, 7)
    rest = values - high
    middle = lax.reduce_precision(rest, 8, 7)
    low = rest - middle
    return [part.astype(BF16) for part in (high, middle, low)]


def dot_nt(left, right, precision=None):
    return lax.dot_general(
        left, right, (((1,), (1,)), ((), ())), precision=precision, preferred_element_type=F32
    )


def dot_nn(left, right, precision=None):
    return lax.dot_general(
        left, right, (((1,), (0,)), ((), ())), precision=precision, preferred_element_type=F32
    )


def dot_tn(left, right, precision=None):
    return lax.dot_general(
        left, right, (((0,), (0,)), ((), ())), precision=precision, preferred_element_type=F32
    )


def split(values):
    high = values.astype(BF16)
    rest = values - high.astype(F32)
    middle = rest.astype(BF16)
    return high, middle, (rest - middle.astype(F32)).astype(BF16)


def extended(rows, left):
    wide = rows.astype(F32)
    lane = lax.broadcasted_iota(jnp.int32, wide.shape, 1)
    parts = split(jnp.sum(wide * wide, axis=1, keepdims=True) * (-1.0 / 64.0))
    first, ones = (0, 3) if left else (3, 0)
    tail = jnp.where((lane >= ones) & (lane < ones + 3), 1.0, 0.0)
    for k in range(3):
        tail = jnp.where(lane == first + k, parts[k].astype(F32), tail)
    head = (wide * 0.03125).astype(BF16) if left else rows
    return jnp.concatenate([head, tail.astype(BF16)], axis=1)


def stacked_dot(dot, values, wide):
    count = values.shape[0]
    parts = jnp.concatenate(split(values), axis=0)
    a = dot(parts, wide[0])
    b = dot(parts[:2 * count], wide[1])
    c = dot(parts[:count], wide[2])
    return a[:count] + ((a[count:2 * count] + b[:count]) + (a[2 * count:] + b[count:] + c))


def eliminate(groups):
    order = len(groups) * GROUP
    lane = lax.broadcasted_iota(jnp.int32, (GROUP, order), 1)
    sub = lax.broadcasted_iota(jnp.int32, (GROUP, order), 0)
    groups = list(groups)
    for first in range(0, order, STRIDE):
        at = first // GROUP
        cols = [None] * len(groups)
        for g in range(at, len(groups)):
            cols[g] = [
                jnp.broadcast_to(groups[g][:, first + j:first + j + 1], (GROUP, order))
                for j in range(STRIDE)
            ]
        home = groups[at]
        own = cols[at]
        rows, inverses, steps = [], [], []
        for j in range(STRIDE):
            r = first % GROUP + j
            inverse = 1.0 / jnp.broadcast_to(own[j][r:r + 1, :], (GROUP, order))
            mult = jnp.where(sub > r, own[j] * inverse, 0.0)
            steps.append(
                [
                    jnp.broadcast_to(own[l][r:r + 1, :], (GROUP, order))
                    for l in range(j + 1, STRIDE)
                ]
            )
            for l in range(j + 1, STRIDE):
                own[l] = own[l] - mult * steps[j][l - j - 1]
            row = jnp.where(
                lane == first + j, 1.0, jnp.broadcast_to(home[r:r + 1, :], (GROUP, order))
            )
            home = jnp.where((lane == first + j) & (sub > r), 0.0, home) - mult * row
            rows.append(jnp.where((lane > first + j) & (lane < first + STRIDE), 0.0, row))
            inverses.append(inverse)
        groups[at] = home
        for g in range(at + 1, len(groups)):
            col = cols[g]
            value = jnp.where((lane >= first) & (lane < first + STRIDE), 0.0, groups[g])
            for j in range(STRIDE):
                mult = col[j] * inverses[j]
                for l in range(j + 1, STRIDE):
                    col[l] = col[l] - mult * steps[j][l - j - 1]
                value = value - mult * rows[j]
            groups[g] = value
    return groups


def inverse_of_block(diag):
    if INTERPRET:
        return jnp.linalg.inv(jnp.linalg.cholesky(diag))
    groups = eliminate([diag[g:g + GROUP, :] for g in range(0, BLOCK, GROUP)])
    done = jnp.concatenate(groups, axis=0)
    row = lax.broadcasted_iota(jnp.int32, (BLOCK, BLOCK), 0)
    col = lax.broadcasted_iota(jnp.int32, (BLOCK, BLOCK), 1)
    pivots = jnp.sum(jnp.where(row == col, done, 0.0), axis=1, keepdims=True)
    unit = jnp.where(col < row, done, jnp.where(col == row, 1.0, 0.0))
    return unit * lax.rsqrt(pivots)


def inverse_factor(work_ref):
    order = work_ref.shape[0]

    def stage(j, carry):
        start = pl.multiple_of(j * BLOCK, BLOCK)
        here = pl.ds(start, BLOCK)
        local = inverse_of_block(work_ref[here, here])
        strip = dot_nn(local, work_ref[here, :], HIGHEST)
        lane = lax.broadcasted_iota(jnp.int32, strip.shape, 1)
        upper = split(jnp.where(lane >= start + BLOCK, strip, 0.0))
        work_ref[here, :] = strip
        work_ref[here, here] = local
        strip = split(work_ref[here, :])
        below = lax.broadcasted_iota(jnp.int32, (order, BLOCK), 0) >= start + BLOCK
        work_ref[:, here] = jnp.where(below, 0.0, work_ref[:, here])
        high_mid = jnp.concatenate(upper[:2], axis=0)
        work_ref[...] = work_ref[...] - (
            dot_tn(high_mid, jnp.concatenate([strip[0], strip[0]], axis=0))
            + (
                dot_tn(high_mid, jnp.concatenate([strip[1], strip[1]], axis=0))
                + dot_tn(
                    jnp.concatenate([upper[0], upper[2]], axis=0),
                    jnp.concatenate([strip[2], strip[0]], axis=0),
                )
            )
        )
        return carry

    lax.fori_loop(0, order // BLOCK, stage, 0)
    row = lax.broadcasted_iota(jnp.int32, (order, order), 0)
    col = lax.broadcasted_iota(jnp.int32, (order, order), 1)
    return jnp.where(col <= row, work_ref[...], 0.0)


def unit_matrix(order, scale):
    row = lax.broadcasted_iota(jnp.int32, (order, order), 0)
    col = lax.broadcasted_iota(jnp.int32, (order, order), 1)
    return jnp.where(row == col, scale, 0.0)


def joined(ref):
    return jnp.concatenate([ref[i] for i in range(ref.shape[0])], axis=1)


def pivots_body(picked_ref, inv_ref, work_ref):
    picked = picked_ref[...]
    right = extended(picked, False)
    work_ref[...] = (
        jnp.exp(dot_nt(extended(picked, True), right)) + unit_matrix(picked.shape[0], JITTER)
    )
    inv_ref[...] = inverse_factor(work_ref)


def setup_body(
    inv_ref, picked_ref, keys_ref, targets_ref,
    high_ref, mid_ref, low_ref, key_ref, out_ref, pack_ref,
):
    piv = inv_ref.shape[0]
    chunks = out_ref.shape[0]
    right = extended(picked_ref[...], False)
    inverse = inv_ref[...]
    key_ref[...] = extended(keys_ref[...], True)
    wide = dot_nt(jnp.exp(dot_nt(key_ref[...], right)), inverse, HIGHEST)
    parts = split(wide)
    high_ref[...] = parts[0]
    mid_ref[...] = parts[1]
    low_ref[...] = parts[2]
    at = 0
    for i in range(piv // BLOCK):
        strip = dot_tn(
            wide[:, i * BLOCK:(i + 1) * BLOCK], wide[:, :(i + 1) * BLOCK], HIGHEST
        )
        for j in range(i + 1):
            pack_ref[at:at + BLOCK, :] = strip[:, j * BLOCK:(j + 1) * BLOCK]
            at += BLOCK
    targets = joined(targets_ref)
    proj = dot_nn(targets, wide, HIGHEST)
    part = at // chunks
    per = proj.shape[0] // chunks
    split_by = piv // BLOCK
    for i in range(chunks):
        out_ref[i, 0:part, :] = pack_ref[i * part:(i + 1) * part, :]
        for p in range(per):
            row = i * per + p
            for k in range(split_by):
                out_ref[i, part + p * split_by + k, :] = proj[row, k * BLOCK:(k + 1) * BLOCK]


def gram_solve(proj, inverse):
    return stacked_dot(dot_nn, stacked_dot(dot_nt, proj, inverse), inverse)


def product(direction, key_ref, row_ref, out_ref):
    keys = key_ref.shape[0]
    count = direction.shape[0]
    parts = jnp.concatenate(split(direction), axis=0)
    chunk = 256

    for first in range(0, row_ref.shape[0], chunk):
        rows = row_ref[first:first + chunk, :]
        total = jnp.zeros((count, chunk), F32)
        for start in range(0, keys, chunk):
            values = jnp.exp(dot_nt(key_ref[start:start + chunk, :], rows))
            high = values.astype(BF16)
            low = (values - high.astype(F32)).astype(BF16)
            a = dot_nn(parts[:, start:start + chunk], high)
            b = dot_nn(parts[:2 * count, start:start + chunk], low)
            total = total + (
                a[:count] + ((a[count:2 * count] + b[:count]) + (a[2 * count:] + b[count:]))
            )
        for k in range(chunk // BLOCK):
            out_ref[first // BLOCK + k] = total[:, k * BLOCK:(k + 1) * BLOCK]


def next_direction(residual, coef, wide):
    return (residual - stacked_dot(dot_nt, coef, wide)) * (1.0 / NOISE)


def gram_body(packed_ref, inv_ref, proj_ref, work_ref, pack_ref):
    piv = work_ref.shape[0]
    chunks = packed_ref.shape[0]
    split_by = piv // BLOCK
    part = split_by * (split_by + 1) // 2 * BLOCK // chunks
    per = proj_ref.shape[0] // chunks
    for i in range(chunks):
        pack_ref[i * part:(i + 1) * part, :] = packed_ref[i, 0:part, :]
        for p in range(per):
            row = i * per + p
            for k in range(split_by):
                proj_ref[row, k * BLOCK:(k + 1) * BLOCK] = packed_ref[i, part + p * split_by + k, :]
    at = 0
    for i in range(split_by):
        for j in range(i + 1):
            piece = pack_ref[at:at + BLOCK, :]
            work_ref[i * BLOCK:(i + 1) * BLOCK, j * BLOCK:(j + 1) * BLOCK] = piece
            if j < i:
                work_ref[j * BLOCK:(j + 1) * BLOCK, i * BLOCK:(i + 1) * BLOCK] = piece.T
            at += BLOCK
    work_ref[...] = work_ref[...] + unit_matrix(piv, NOISE)
    inv_ref[...] = inverse_factor(work_ref)


def begin_body(
    proj_ref, inv_ref, res_ref, high_ref, mid_ref, low_ref, key_ref,
    points_ref, dir_ref, row_ref, out_ref,
):
    chips = points_ref.shape[0]
    for i in range(chips):
        for k in range(2):
            at = (k * chips + i) * BLOCK
            row_ref[at:at + BLOCK, :] = extended(points_ref[i, k * BLOCK:(k + 1) * BLOCK, :], False)
    coef = gram_solve(proj_ref[...], split(inv_ref[...]))
    direction = next_direction(joined(res_ref), coef, (high_ref[...], mid_ref[...], low_ref[...]))
    for i in range(dir_ref.shape[0]):
        dir_ref[i] = direction[:, i * BLOCK:(i + 1) * BLOCK]
    product(direction, key_ref, row_ref, out_ref)


def project_body(image_ref, res_ref, dir_ref, high_ref, mid_ref, low_ref, out_ref):
    image = joined(image_ref)
    residual = joined(res_ref)
    direction = joined(dir_ref)
    piv = high_ref.shape[1]
    out_ref[:, :piv] = stacked_dot(dot_nn, image, (high_ref[...], mid_ref[...], low_ref[...]))
    curve = jnp.sum(direction * image, axis=1, keepdims=True)
    cross = jnp.sum(residual * image, axis=1, keepdims=True)
    own = jnp.sum(image * image, axis=1, keepdims=True)
    along = jnp.sum(direction * residual, axis=1, keepdims=True)
    squares = jnp.sum(residual * residual, axis=1, keepdims=True)
    lane = lax.broadcasted_iota(jnp.int32, (image.shape[0], BLOCK), 1)
    sums = jnp.where(lane == 0, curve, jnp.where(lane == 1, cross, own))
    out_ref[:, piv:] = jnp.where(lane == 3, along, jnp.where(lane == 4, squares, sums))


def advance_body(
    packed_ref, image_ref, res_ref, dir_ref, sol_ref, proj_ref,
    inv_ref, high_ref, mid_ref, low_ref, key_ref, row_ref,
    new_res, new_dir, new_sol, new_proj, out_ref,
):
    piv = proj_ref.shape[1]
    total = packed_ref[...]
    inner = total[:, piv + 3:piv + 4]
    alpha = inner / total[:, piv:piv + 1]
    squares = (
        total[:, piv + 4:piv + 5] - 2.0 * alpha * total[:, piv + 1:piv + 2]
        + alpha * alpha * total[:, piv + 2:piv + 3]
    )
    proj = proj_ref[...] - alpha * total[:, :piv]
    coef = gram_solve(proj, split(inv_ref[...]))
    inner_next = (squares - jnp.sum(proj * coef, axis=1, keepdims=True)) * (1.0 / NOISE)
    beta = inner_next / inner
    new_proj[...] = proj
    direction = joined(dir_ref)
    residual = joined(res_ref) - alpha * joined(image_ref)
    solution = joined(sol_ref) + alpha * direction
    direction = (
        next_direction(residual, coef, (high_ref[...], mid_ref[...], low_ref[...]))
        + beta * direction
    )
    for i in range(new_dir.shape[0]):
        new_res[i] = residual[:, i * BLOCK:(i + 1) * BLOCK]
        new_dir[i] = direction[:, i * BLOCK:(i + 1) * BLOCK]
        new_sol[i] = solution[:, i * BLOCK:(i + 1) * BLOCK]
    product(direction, key_ref, row_ref, out_ref)


def call(body, name, outs, scratch, *args, seconds=10e-6):
    return pl.pallas_call(
        body,
        out_shape=[jax.ShapeDtypeStruct(shape, dtype) for shape, dtype in outs],
        scratch_shapes=scratch,
        compiler_params=pltpu.CompilerParams(vmem_limit_bytes=48 << 20),
        cost_estimate=pl.CostEstimate(
            flops=int(seconds * 1e15), bytes_accessed=int(seconds * 3e12), transcendentals=0
        ),
        interpret=INTERPRET,
        name=name,
    )(*args)


def per_device(points, targets, pivots):
    own = points.shape[0]
    columns = targets.shape[1]
    u_size, chips = lax.axis_size(U), lax.axis_size(CHIPS)
    u_at, core = lax.axis_index(U), lax.axis_index("c")
    v_size = 2 * chips
    flat_pivots = pivots.reshape(-1)
    piv = flat_pivots.shape[0]
    part = piv // v_size
    per = columns // v_size

    place = jnp.zeros((), jnp.int32)
    for axis in ALL:
        place = place * lax.axis_size(axis) + lax.axis_index(axis)
    own_ids = place * own + jnp.arange(own, dtype=jnp.int32)
    owned = (flat_pivots[:, None] == own_ids[None, :]).astype(BF16)
    held = jnp.dot(owned, points, preferred_element_type=F32).astype(BF16)
    held = half(held, core) + partner(half(held, 1 - core))
    picked = swap(held.reshape(chips, part, -1), CHIPS)
    picked = jnp.sum(picked.astype(F32), axis=0).astype(BF16)
    picked = jnp.sum(share(picked, U).astype(F32), axis=0).astype(BF16)
    picked = share(picked, CHIPS)
    picked = core_first(picked, partner(picked)).reshape(piv, -1)

    both_points = jnp.concatenate([points, partner(points)], axis=0)
    points, targets, picked, both_points = lax.optimization_barrier(
        (points, targets, picked, both_points)
    )
    packed = share(jnp.concatenate([points] + three_parts(targets.T), axis=0), U)
    key_points = packed[:, :own].reshape(u_size * own, -1)
    parts = packed[:, own:].astype(F32).reshape(u_size, 3, columns, own)
    residual = parts[:, 0] + parts[:, 1] + parts[:, 2]
    piv_inverse = call(
        pivots_body, "pivots_factor", [((piv, piv), F32)], [pltpu.VMEM((piv, piv), F32)], picked,
        seconds=22e-6,
    )[0]

    keys = key_points.shape[0]
    lower = piv // BLOCK * (piv // BLOCK + 1) // 2 * BLOCK
    height = (lower // v_size + per * (piv // BLOCK) + 7) // 8 * 8
    work = [pltpu.VMEM((piv, piv), F32), pltpu.VMEM((lower, BLOCK), F32)]
    *wide, key_left, packed = call(
        setup_body, "setup_factor",
        [((keys, piv), BF16)] * 3
        + [((keys, 2 * BLOCK), BF16), ((v_size, height, BLOCK), F32)],
        work[1:], piv_inverse, picked, key_points, residual,
    )
    factor = lax.dynamic_slice_in_dim(wide[0], u_at * own, own, 0)
    packed = jnp.sum(swap(half(packed, core) + partner(half(packed, 1 - core)), CHIPS), axis=0)
    packed = share(packed, CHIPS)
    packed = core_first(packed, partner(packed))

    state = ((u_size, columns, own), F32)
    partial_shape = ((v_size, columns, own), F32)
    both_points, packed = lax.optimization_barrier((both_points, packed))
    row_points = share(both_points, CHIPS)
    inverse, projection = call(
        gram_body, "gram_factor", [((piv, piv), F32), ((columns, piv), F32)], work, packed,
        seconds=22e-6,
    )
    direction, row_right, partial = call(
        begin_body, "begin", [state, ((v_size * own, 2 * BLOCK), BF16), partial_shape], [],
        projection, inverse, residual, *wide, key_left, row_points,
    )
    solution_now = jnp.zeros(state[0], F32)
    for step in range(ITERS):
        direction_own = lax.dynamic_index_in_dim(direction, u_at, 0, keepdims=False)
        blocks = partial[:chips] + partner(partial[chips:])
        image_own = jnp.sum(swap(blocks, CHIPS), axis=0) + NOISE * direction_own
        if step + 1 == ITERS:
            break
        image = share(image_own, U)
        packed = call(
            project_body, "project", [((columns, piv + BLOCK), F32)], [],
            image, residual, direction, *wide,
        )[0]
        packed = half(packed, core) + partner(half(packed, 1 - core))
        packed = packed + other_of_two(packed, CHIPS[1])
        packed = jnp.sum(share(packed, (CHIPS[0], CHIPS[2])), axis=0)
        packed = core_first(packed, partner(packed))
        residual, direction, solution_now, projection, partial = call(
            advance_body, "advance",
            [state, state, state, ((columns, piv), F32), partial_shape], [],
            packed, image, residual, direction, solution_now, projection,
            inverse, *wide, key_left, row_right,
        )
    solution_own = lax.dynamic_index_in_dim(solution_now, u_at, 0, keepdims=False)
    residual_own = lax.dynamic_index_in_dim(residual, u_at, 0, keepdims=False)
    sums = jnp.concatenate(
        [
            jnp.sum(direction_own * image_own, axis=1),
            jnp.sum(direction_own * residual_own, axis=1),
            jnp.zeros((BLOCK - 2 * columns,), F32),
        ]
    )
    sums = jnp.sum(share(sums[None], ALL), axis=(0, 1))
    alpha = (sums[columns:2 * columns] / sums[:columns])[:, None]
    solution_own = solution_own + alpha * direction_own
    residual_own = residual_own - alpha * image_own
    return (factor, solution_own.T, residual_own.T)


def solution(mesh):
    sizes = (4, 8, 2, 2, 2) if mesh.devices.size == 256 else (1, 2, 2, 2, 2)
    grid = Mesh(mesh.devices.reshape(sizes), ALL)
    return jax.shard_map(
        per_device,
        mesh=grid,
        in_specs=(P(ALL, None), P(ALL, None), P()),
        out_specs=(P(ALL, None), P(ALL, None), P(ALL, None)),
        check_vma=False,
    )
```

```python
import functools

import jax
import jax.numpy as jnp
from jax import lax
from jax.experimental import pallas as pl
from jax.experimental.pallas import tpu as pltpu
from jax.sharding import Mesh, PartitionSpec as P

ITERS = 3
NOISE = 0.5
JITTER = 0.05
HIGHEST = lax.Precision.HIGHEST
INTERPRET = False
GROUP = 8
STRIDE = 8
BLOCK = 128
F32 = jnp.float32
BF16 = jnp.bfloat16

U = ("z",)
CHIPS = ("x", "yh", "yl")
ALL = ("x", "z", "yh", "yl", "c")


def swap(blocks, axes):
    return lax.all_to_all(blocks, axes, 0, 0, tiled=False)


def share(block, axes):
    count = lax.axis_size(axes)
    return swap(jnp.broadcast_to(block[None], (count,) + block.shape), axes)


def other_of_two(values, axis):
    count = lax.axis_size(axis)
    return lax.ppermute(values, axis, [(i, (i + 1) % count) for i in range(count)])


def partner(values):
    return other_of_two(values, "c")


def core_first(mine, other):
    first = lax.axis_index("c") == 0
    return jnp.concatenate([jnp.where(first, mine, other), jnp.where(first, other, mine)], axis=0)


def half(values, at):
    count = values.shape[0] // 2
    return lax.dynamic_slice_in_dim(values, at * count, count, 0)


def three_parts(values):
    high = lax.reduce_precision(values, 8, 7)
    rest = values - high
    middle = lax.reduce_precision(rest, 8, 7)
    low = rest - middle
    return [part.astype(BF16) for part in (high, middle, low)]


def dot_nt(left, right, precision=None):
    return lax.dot_general(
        left, right, (((1,), (1,)), ((), ())), precision=precision, preferred_element_type=F32
    )


def dot_nn(left, right, precision=None):
    return lax.dot_general(
        left, right, (((1,), (0,)), ((), ())), precision=precision, preferred_element_type=F32
    )


def dot_tn(left, right, precision=None):
    return lax.dot_general(
        left, right, (((0,), (0,)), ((), ())), precision=precision, preferred_element_type=F32
    )


def split(values):
    high = values.astype(BF16)
    rest = values - high.astype(F32)
    middle = rest.astype(BF16)
    return high, middle, (rest - middle.astype(F32)).astype(BF16)


def extended(rows, left):
    wide = rows.astype(F32)
    lane = lax.broadcasted_iota(jnp.int32, wide.shape, 1)
    parts = split(jnp.sum(wide * wide, axis=1, keepdims=True) * (-1.0 / 64.0))
    first, ones = (0, 3) if left else (3, 0)
    tail = jnp.where((lane >= ones) & (lane < ones + 3), 1.0, 0.0)
    for k in range(3):
        tail = jnp.where(lane == first + k, parts[k].astype(F32), tail)
    head = (wide * 0.03125).astype(BF16) if left else rows
    return jnp.concatenate([head, tail.astype(BF16)], axis=1)


def stacked_dot(dot, values, wide):
    count = values.shape[0]
    parts = jnp.concatenate(split(values), axis=0)
    a = dot(parts, wide[0])
    b = dot(parts[:2 * count], wide[1])
    c = dot(parts[:count], wide[2])
    return a[:count] + ((a[count:2 * count] + b[:count]) + (a[2 * count:] + b[count:] + c))


def eliminate(groups):
    order = len(groups) * GROUP
    lane = lax.broadcasted_iota(jnp.int32, (GROUP, order), 1)
    sub = lax.broadcasted_iota(jnp.int32, (GROUP, order), 0)
    groups = list(groups)
    for first in range(0, order, STRIDE):
        at = first // GROUP
        cols = [None] * len(groups)
        for g in range(at, len(groups)):
            cols[g] = [
                jnp.broadcast_to(groups[g][:, first + j:first + j + 1], (GROUP, order))
                for j in range(STRIDE)
            ]
        home = groups[at]
        own = cols[at]
        rows, inverses, steps = [], [], []
        for j in range(STRIDE):
            r = first % GROUP + j
            inverse = 1.0 / jnp.broadcast_to(own[j][r:r + 1, :], (GROUP, order))
            mult = jnp.where(sub > r, own[j] * inverse, 0.0)
            steps.append(
                [
                    jnp.broadcast_to(own[l][r:r + 1, :], (GROUP, order))
                    for l in range(j + 1, STRIDE)
                ]
            )
            for l in range(j + 1, STRIDE):
                own[l] = own[l] - mult * steps[j][l - j - 1]
            row = jnp.where(
                lane == first + j, 1.0, jnp.broadcast_to(home[r:r + 1, :], (GROUP, order))
            )
            home = jnp.where((lane == first + j) & (sub > r), 0.0, home) - mult * row
            rows.append(jnp.where((lane > first + j) & (lane < first + STRIDE), 0.0, row))
            inverses.append(inverse)
        groups[at] = home
        for g in range(at + 1, len(groups)):
            col = cols[g]
            value = jnp.where((lane >= first) & (lane < first + STRIDE), 0.0, groups[g])
            for j in range(STRIDE):
                mult = col[j] * inverses[j]
                for l in range(j + 1, STRIDE):
                    col[l] = col[l] - mult * steps[j][l - j - 1]
                value = value - mult * rows[j]
            groups[g] = value
    return groups


def inverse_of_block(diag):
    if INTERPRET:
        return jnp.linalg.inv(jnp.linalg.cholesky(diag))
    groups = eliminate([diag[g:g + GROUP, :] for g in range(0, BLOCK, GROUP)])
    done = jnp.concatenate(groups, axis=0)
    row = lax.broadcasted_iota(jnp.int32, (BLOCK, BLOCK), 0)
    col = lax.broadcasted_iota(jnp.int32, (BLOCK, BLOCK), 1)
    pivots = jnp.sum(jnp.where(row == col, done, 0.0), axis=1, keepdims=True)
    unit = jnp.where(col < row, done, jnp.where(col == row, 1.0, 0.0))
    return unit * lax.rsqrt(pivots)


def inverse_factor(work_ref):
    order = work_ref.shape[0]

    def stage(j, carry):
        start = pl.multiple_of(j * BLOCK, BLOCK)
        here = pl.ds(start, BLOCK)
        local = inverse_of_block(work_ref[here, here])
        strip = dot_nn(local, work_ref[here, :], HIGHEST)
        lane = lax.broadcasted_iota(jnp.int32, strip.shape, 1)
        upper = split(jnp.where(lane >= start + BLOCK, strip, 0.0))
        work_ref[here, :] = strip
        work_ref[here, here] = local
        strip = split(work_ref[here, :])
        below = lax.broadcasted_iota(jnp.int32, (order, BLOCK), 0) >= start + BLOCK
        work_ref[:, here] = jnp.where(below, 0.0, work_ref[:, here])
        high_mid = jnp.concatenate(upper[:2], axis=0)
        work_ref[...] = work_ref[...] - (
            dot_tn(high_mid, jnp.concatenate([strip[0], strip[0]], axis=0))
            + (
                dot_tn(high_mid, jnp.concatenate([strip[1], strip[1]], axis=0))
                + dot_tn(
                    jnp.concatenate([upper[0], upper[2]], axis=0),
                    jnp.concatenate([strip[2], strip[0]], axis=0),
                )
            )
        )
        return carry

    lax.fori_loop(0, order // BLOCK, stage, 0)
    row = lax.broadcasted_iota(jnp.int32, (order, order), 0)
    col = lax.broadcasted_iota(jnp.int32, (order, order), 1)
    return jnp.where(col <= row, work_ref[...], 0.0)


def unit_matrix(order, scale):
    row = lax.broadcasted_iota(jnp.int32, (order, order), 0)
    col = lax.broadcasted_iota(jnp.int32, (order, order), 1)
    return jnp.where(row == col, scale, 0.0)


def joined(ref):
    return jnp.concatenate([ref[i] for i in range(ref.shape[0])], axis=1)


def pivots_body(picked_ref, inv_ref, work_ref):
    picked = picked_ref[...]
    right = extended(picked, False)
    work_ref[...] = (
        jnp.exp(dot_nt(extended(picked, True), right)) + unit_matrix(picked.shape[0], JITTER)
    )
    inv_ref[...] = inverse_factor(work_ref)


def setup_body(
    inv_ref, picked_ref, keys_ref, targets_ref,
    high_ref, mid_ref, low_ref, key_ref, out_ref, pack_ref,
):
    piv = inv_ref.shape[0]
    chunks = out_ref.shape[0]
    right = extended(picked_ref[...], False)
    inverse = inv_ref[...]
    key_ref[...] = extended(keys_ref[...], True)
    wide = dot_nt(jnp.exp(dot_nt(key_ref[...], right)), inverse, HIGHEST)
    parts = split(wide)
    high_ref[...] = parts[0]
    mid_ref[...] = parts[1]
    low_ref[...] = parts[2]
    at = 0
    for i in range(piv // BLOCK):
        strip = dot_tn(
            wide[:, i * BLOCK:(i + 1) * BLOCK], wide[:, :(i + 1) * BLOCK], HIGHEST
        )
        for j in range(i + 1):
            pack_ref[at:at + BLOCK, :] = strip[:, j * BLOCK:(j + 1) * BLOCK]
            at += BLOCK
    targets = joined(targets_ref)
    proj = dot_nn(targets, wide, HIGHEST)
    part = at // chunks
    per = proj.shape[0] // chunks
    split_by = piv // BLOCK
    for i in range(chunks):
        out_ref[i, 0:part, :] = pack_ref[i * part:(i + 1) * part, :]
        for p in range(per):
            row = i * per + p
            for k in range(split_by):
                out_ref[i, part + p * split_by + k, :] = proj[row, k * BLOCK:(k + 1) * BLOCK]


def gram_solve(proj, inverse):
    return stacked_dot(dot_nn, stacked_dot(dot_nt, proj, inverse), inverse)


def product(direction, key_ref, row_ref, out_ref):
    keys = key_ref.shape[0]
    count = direction.shape[0]
    parts = jnp.concatenate(split(direction), axis=0)
    chunk = 256

    for first in range(0, row_ref.shape[0], chunk):
        rows = row_ref[first:first + chunk, :]
        total = jnp.zeros((count, chunk), F32)
        for start in range(0, keys, chunk):
            values = jnp.exp(dot_nt(key_ref[start:start + chunk, :], rows))
            high = values.astype(BF16)
            low = (values - high.astype(F32)).astype(BF16)
            a = dot_nn(parts[:, start:start + chunk], high)
            b = dot_nn(parts[:2 * count, start:start + chunk], low)
            total = total + (
                a[:count] + ((a[count:2 * count] + b[:count]) + (a[2 * count:] + b[count:]))
            )
        for k in range(chunk // BLOCK):
            out_ref[first // BLOCK + k] = total[:, k * BLOCK:(k + 1) * BLOCK]


def next_direction(residual, coef, wide):
    return (residual - stacked_dot(dot_nt, coef, wide)) * (1.0 / NOISE)


def gram_body(packed_ref, inv_ref, proj_ref, work_ref, pack_ref):
    piv = work_ref.shape[0]
    chunks = packed_ref.shape[0]
    split_by = piv // BLOCK
    part = split_by * (split_by + 1) // 2 * BLOCK // chunks
    per = proj_ref.shape[0] // chunks
    for i in range(chunks):
        pack_ref[i * part:(i + 1) * part, :] = packed_ref[i, 0:part, :]
        for p in range(per):
            row = i * per + p
            for k in range(split_by):
                proj_ref[row, k * BLOCK:(k + 1) * BLOCK] = packed_ref[i, part + p * split_by + k, :]
    at = 0
    for i in range(split_by):
        for j in range(i + 1):
            piece = pack_ref[at:at + BLOCK, :]
            work_ref[i * BLOCK:(i + 1) * BLOCK, j * BLOCK:(j + 1) * BLOCK] = piece
            if j < i:
                work_ref[j * BLOCK:(j + 1) * BLOCK, i * BLOCK:(i + 1) * BLOCK] = piece.T
            at += BLOCK
    work_ref[...] = work_ref[...] + unit_matrix(piv, NOISE)
    inv_ref[...] = inverse_factor(work_ref)


def begin_body(
    proj_ref, inv_ref, res_ref, high_ref, mid_ref, low_ref, key_ref,
    points_ref, dir_ref, row_ref, out_ref,
):
    chips = points_ref.shape[0]
    for i in range(chips):
        for k in range(2):
            at = (k * chips + i) * BLOCK
            row_ref[at:at + BLOCK, :] = extended(points_ref[i, k * BLOCK:(k + 1) * BLOCK, :], False)
    coef = gram_solve(proj_ref[...], split(inv_ref[...]))
    direction = next_direction(joined(res_ref), coef, (high_ref[...], mid_ref[...], low_ref[...]))
    for i in range(dir_ref.shape[0]):
        dir_ref[i] = direction[:, i * BLOCK:(i + 1) * BLOCK]
    product(direction, key_ref, row_ref, out_ref)


def project_body(image_ref, res_ref, dir_ref, high_ref, mid_ref, low_ref, out_ref):
    image = joined(image_ref)
    residual = joined(res_ref)
    direction = joined(dir_ref)
    piv = high_ref.shape[1]
    out_ref[:, :piv] = stacked_dot(dot_nn, image, (high_ref[...], mid_ref[...], low_ref[...]))
    curve = jnp.sum(direction * image, axis=1, keepdims=True)
    cross = jnp.sum(residual * image, axis=1, keepdims=True)
    own = jnp.sum(image * image, axis=1, keepdims=True)
    along = jnp.sum(direction * residual, axis=1, keepdims=True)
    squares = jnp.sum(residual * residual, axis=1, keepdims=True)
    lane = lax.broadcasted_iota(jnp.int32, (image.shape[0], BLOCK), 1)
    sums = jnp.where(lane == 0, curve, jnp.where(lane == 1, cross, own))
    out_ref[:, piv:] = jnp.where(lane == 3, along, jnp.where(lane == 4, squares, sums))


def advance_body(
    packed_ref, image_ref, res_ref, dir_ref, sol_ref, proj_ref,
    inv_ref, high_ref, mid_ref, low_ref, key_ref, row_ref,
    new_res, new_dir, new_sol, new_proj, out_ref,
):
    piv = proj_ref.shape[1]
    total = packed_ref[...]
    inner = total[:, piv + 3:piv + 4]
    alpha = inner / total[:, piv:piv + 1]
    squares = (
        total[:, piv + 4:piv + 5] - 2.0 * alpha * total[:, piv + 1:piv + 2]
        + alpha * alpha * total[:, piv + 2:piv + 3]
    )
    proj = proj_ref[...] - alpha * total[:, :piv]
    coef = gram_solve(proj, split(inv_ref[...]))
    inner_next = (squares - jnp.sum(proj * coef, axis=1, keepdims=True)) * (1.0 / NOISE)
    beta = inner_next / inner
    new_proj[...] = proj
    direction = joined(dir_ref)
    residual = joined(res_ref) - alpha * joined(image_ref)
    solution = joined(sol_ref) + alpha * direction
    direction = (
        next_direction(residual, coef, (high_ref[...], mid_ref[...], low_ref[...]))
        + beta * direction
    )
    for i in range(new_dir.shape[0]):
        new_res[i] = residual[:, i * BLOCK:(i + 1) * BLOCK]
        new_dir[i] = direction[:, i * BLOCK:(i + 1) * BLOCK]
        new_sol[i] = solution[:, i * BLOCK:(i + 1) * BLOCK]
    product(direction, key_ref, row_ref, out_ref)


def call(body, name, outs, scratch, *args, seconds=10e-6):
    return pl.pallas_call(
        body,
        out_shape=[jax.ShapeDtypeStruct(shape, dtype) for shape, dtype in outs],
        scratch_shapes=scratch,
        compiler_params=pltpu.CompilerParams(vmem_limit_bytes=48 << 20),
        cost_estimate=pl.CostEstimate(
            flops=int(seconds * 1e15), bytes_accessed=int(seconds * 3e12), transcendentals=0
        ),
        interpret=INTERPRET,
        name=name,
    )(*args)


def per_device(points, targets, pivots):
    own = points.shape[0]
    columns = targets.shape[1]
    u_size, chips = lax.axis_size(U), lax.axis_size(CHIPS)
    u_at, core = lax.axis_index(U), lax.axis_index("c")
    v_size = 2 * chips
    flat_pivots = pivots.reshape(-1)
    piv = flat_pivots.shape[0]
    part = piv // v_size
    per = columns // v_size

    place = jnp.zeros((), jnp.int32)
    for axis in ALL:
        place = place * lax.axis_size(axis) + lax.axis_index(axis)
    own_ids = place * own + jnp.arange(own, dtype=jnp.int32)
    owned = (flat_pivots[:, None] == own_ids[None, :]).astype(BF16)
    held = jnp.dot(owned, points, preferred_element_type=F32).astype(BF16)
    held = half(held, core) + partner(half(held, 1 - core))
    picked = swap(held.reshape(chips, part, -1), CHIPS)
    picked = jnp.sum(picked.astype(F32), axis=0).astype(BF16)
    picked = jnp.sum(share(picked, U).astype(F32), axis=0).astype(BF16)
    picked = share(picked, CHIPS)
    picked = core_first(picked, partner(picked)).reshape(piv, -1)

    both_points = jnp.concatenate([points, partner(points)], axis=0)
    both_points = jnp.broadcast_to(both_points[None], (chips,) + both_points.shape)
    packed = jnp.concatenate([points] + three_parts(targets.T), axis=0)
    packed = jnp.broadcast_to(packed[None], (u_size,) + packed.shape)
    picked, packed, both_points = lax.optimization_barrier((picked, packed, both_points))
    packed = swap(packed, U)
    key_points = packed[:, :own].reshape(u_size * own, -1)
    parts = packed[:, own:].astype(F32).reshape(u_size, 3, columns, own)
    residual = parts[:, 0] + parts[:, 1] + parts[:, 2]
    piv_inverse = call(
        pivots_body, "pivots_factor", [((piv, piv), F32)], [pltpu.VMEM((piv, piv), F32)], picked,
        seconds=22e-6,
    )[0]

    keys = key_points.shape[0]
    lower = piv // BLOCK * (piv // BLOCK + 1) // 2 * BLOCK
    height = (lower // v_size + per * (piv // BLOCK) + 7) // 8 * 8
    work = [pltpu.VMEM((piv, piv), F32), pltpu.VMEM((lower, BLOCK), F32)]
    *wide, key_left, packed = call(
        setup_body, "setup_factor",
        [((keys, piv), BF16)] * 3
        + [((keys, 2 * BLOCK), BF16), ((v_size, height, BLOCK), F32)],
        work[1:], piv_inverse, picked, key_points, residual,
    )
    factor = lax.dynamic_slice_in_dim(wide[0], u_at * own, own, 0)
    packed = jnp.sum(swap(half(packed, core) + partner(half(packed, 1 - core)), CHIPS), axis=0)
    packed = share(packed, CHIPS)
    packed = core_first(packed, partner(packed))

    state = ((u_size, columns, own), F32)
    partial_shape = ((v_size, columns, own), F32)
    both_points, packed = lax.optimization_barrier((both_points, packed))
    row_points = swap(both_points, CHIPS)
    inverse, projection = call(
        gram_body, "gram_factor", [((piv, piv), F32), ((columns, piv), F32)], work, packed,
        seconds=22e-6,
    )
    direction, row_right, partial = call(
        begin_body, "begin", [state, ((v_size * own, 2 * BLOCK), BF16), partial_shape], [],
        projection, inverse, residual, *wide, key_left, row_points,
    )
    solution_now = jnp.zeros(state[0], F32)
    for step in range(ITERS):
        direction_own = lax.dynamic_index_in_dim(direction, u_at, 0, keepdims=False)
        blocks = partial[:chips] + partner(partial[chips:])
        image_own = jnp.sum(swap(blocks, CHIPS), axis=0) + NOISE * direction_own
        if step + 1 == ITERS:
            break
        image = share(image_own, U)
        packed = call(
            project_body, "project", [((columns, piv + BLOCK), F32)], [],
            image, residual, direction, *wide,
        )[0]
        packed = half(packed, core) + partner(half(packed, 1 - core))
        packed = packed + other_of_two(packed, CHIPS[1])
        packed = jnp.sum(share(packed, (CHIPS[0], CHIPS[2])), axis=0)
        packed = core_first(packed, partner(packed))
        residual, direction, solution_now, projection, partial = call(
            advance_body, "advance",
            [state, state, state, ((columns, piv), F32), partial_shape], [],
            packed, image, residual, direction, solution_now, projection,
            inverse, *wide, key_left, row_right,
        )
    solution_own = lax.dynamic_index_in_dim(solution_now, u_at, 0, keepdims=False)
    residual_own = lax.dynamic_index_in_dim(residual, u_at, 0, keepdims=False)
    sums = jnp.concatenate(
        [
            jnp.sum(direction_own * image_own, axis=1),
            jnp.sum(direction_own * residual_own, axis=1),
            jnp.zeros((BLOCK - 2 * columns,), F32),
        ]
    )
    sums = jnp.sum(share(sums[None], ALL), axis=(0, 1))
    alpha = (sums[columns:2 * columns] / sums[:columns])[:, None]
    solution_own = solution_own + alpha * direction_own
    residual_own = residual_own - alpha * image_own
    return (factor, solution_own.T, residual_own.T)


def solution(mesh):
    sizes = (4, 8, 2, 2, 2) if mesh.devices.size == 256 else (1, 2, 2, 2, 2)
    grid = Mesh(mesh.devices.reshape(sizes), ALL)
    return jax.shard_map(
        per_device,
        mesh=grid,
        in_specs=(P(ALL, None), P(ALL, None), P()),
        out_specs=(P(ALL, None), P(ALL, None), P(ALL, None)),
        check_vma=False,
    )
```
